512 devices in a mesh: basin: 32 (over y, x, core), member: 16 (over z).
Axes of the slice: x: 4, y: 4, z: 16, core: 2. Of those that a mesh axis runs over, the one named last changes fastest.
Arguments:
- initial_reservoir_levels: float32 [64, 4, 32768], P('member', None, 'basin'), may hold values from 0 to 1
- normalized_catchment_settings: float32 [10, 32768], P(None, 'basin'), may hold values from 0 to 1
- rainfall_member_series: float32 [24, 64, 32768], P(None, 'member', 'basin'), may hold values from 0 to 0.03
- surface_heat_celsius: float32 [24, 32768], P(None, 'basin'), may hold values from -12 to 12
- potential_evapotranspiration: float32 [24, 32768], P(None, 'basin'), may hold values from 0 to 0.01
- gauge_measured_values: float32 [128, 32], P('basin'), may hold values from 0 to 1
- gauge_deviation_sigma: float32 [128, 32], P('basin'), may hold values from 0.05 to 0.5
- gauge_perturbation_draws: float32 [128, 32, 64], P('basin', None, 'member'), may hold values from -6 to 6
- gauge_catchment_position: int32 [128, 32], P('basin'), may hold values from 0 to 255
- gauge_present_flag: int32 [128, 32], P('basin'), may hold values 0 or 1
- adjacent_block_list: int32 [128, 3], replicated, may hold values from 0 to 127, as said below
Outputs:
- analysis: float32 [64, 4, 32768], P('member', None, 'basin')
- discharge_series: float32 [24, 64, 32768], P(None, 'member', 'basin')
The draws below stay inside these ranges and needn't reach their ends.
Inputs may be any that keep to these rules, and one draw needn't show every extreme that they name: `adjacent_block_list`: no block lists itself. Of the 12 entries of any aligned range of 4 blocks, at most 2 point into any one aligned range of 4 blocks, and exactly 2 into some range.
All inputs are finite; a program needn't handle non-finite values. No bound on the sum of `gauge_present_flag` on one device may be relied on, other than what follows from the above.
Results may differ from the reference program's by a relative error of at most 0.0003.
Values sent between devices are 32-bit elements; how exact they have to be, the bound alone decides.
A program may use at most 64 MiB of HBM per device.

```python
import math
import jax
import jax.numpy as jnp
from jax import lax

NB = 256
BLK_DEV = 4
ENSEMBLE_SIZE = 64
LEAD_TIME_LENGTH = 24
OBS = 32
NBR = 3
NPAR = 10
LOCAL = 128
BLOCKS = 128
CATCHMENT_COUNT = 32768
CAP = 2


def draw_adjacent_block_list(key, part):
    device_count = BLOCKS // BLK_DEV
    entries = BLK_DEV * NBR
    key_shift, key_pool, key_order, key_block = jax.random.split(key, 4)
    first_shift = jax.random.randint(key_shift, (), 0, device_count)
    other_shift = (first_shift + 1 + jnp.arange(device_count - 1, dtype=jnp.int32)) % device_count
    shift_pool = jnp.repeat(other_shift, CAP)
    pool_order = jax.random.permutation(key_pool, shift_pool.shape[0])
    remaining = shift_pool[pool_order][:entries - CAP]
    shifts = jnp.concatenate([jnp.full((CAP,), first_shift, dtype=jnp.int32), remaining.astype(jnp.int32)])
    scores = jax.random.randint(key_order, (device_count, entries), 0, 1024) * entries + jnp.arange(entries, dtype=jnp.int32)[None, :]
    placed = jnp.argsort(scores, axis=1)
    device_shift = shifts[placed]
    device_ids = jnp.arange(device_count, dtype=jnp.int32)[:, None]
    owner_dev = (device_ids + device_shift) % device_count
    local_block = jax.random.randint(key_block, (device_count, entries), 0, BLK_DEV)
    home_block = jnp.arange(entries, dtype=jnp.int32)[None, :] // NBR
    clash = (owner_dev == device_ids) & (local_block == home_block)
    local_block = jnp.where(clash, (local_block + 1) % BLK_DEV, local_block)
    return (owner_dev * BLK_DEV + local_block).reshape(BLOCKS, NBR).astype(jnp.int32)


def plant(drawn, key, low, high):
    longest = drawn.shape.index(max(drawn.shape))
    spots = []
    for shift in (0, 1):
        where = [jax.random.randint(jax.random.fold_in(key, axis), (), 0, length) for axis, length in enumerate(drawn.shape)]
        where[longest] = (where[longest] + shift) % drawn.shape[longest]
        spots.append(tuple(where))
    return drawn.at[spots[0]].set(low).at[spots[1]].set(high)


def block_levels(key, dims, cuts, smallest, top_value):
    factor_of = 1.0
    for dim, parts in cuts:
        steps = jax.random.uniform(jax.random.fold_in(jax.random.fold_in(key, 6), dim), (parts,), jnp.float32, smallest / len(cuts), top_value / len(cuts))
        factor_of = factor_of * jnp.repeat(jnp.exp(steps), dims[dim] // parts).reshape((-1,) + (1,) * (len(dims) - 1 - dim))
    return factor_of


def gaussian(rng, extent, deviation, bound, cuts=(), held_as=jnp.bfloat16):
    drawn = jax.random.normal(rng, extent, jnp.float32) * deviation
    if len(cuts) > 0:
        drawn = block_levels(rng, extent, cuts, -0.22, 0.18) * drawn
    return jnp.clip(drawn, min=-bound, max=bound).astype(held_as)


def setup_inputs(seed: int = 0) -> dict:
    key_list = jax.random.split(jax.random.key(seed), 12)
    return {
        "initial_reservoir_levels": jnp.clip(1.0 * jax.random.uniform(key_list[0], (ENSEMBLE_SIZE, 4, CATCHMENT_COUNT), jnp.float32) ** block_levels(key_list[0], (ENSEMBLE_SIZE, 4, CATCHMENT_COUNT), ((0, 16), (2, 32)), -0.2, 0.2), 0.0, 1.0),
        "normalized_catchment_settings": jnp.clip(1.0 * jax.random.uniform(key_list[1], (NPAR, CATCHMENT_COUNT), jnp.float32) ** block_levels(key_list[1], (NPAR, CATCHMENT_COUNT), ((1, 32),), -0.2, 0.2), 0.0, 1.0),
        "rainfall_member_series": jnp.clip(0.03 * jax.random.uniform(key_list[2], (LEAD_TIME_LENGTH, ENSEMBLE_SIZE, CATCHMENT_COUNT), jnp.float32) ** block_levels(key_list[2], (LEAD_TIME_LENGTH, ENSEMBLE_SIZE, CATCHMENT_COUNT), ((1, 16), (2, 32)), -0.2, 0.2), 0.0, 0.03),
        "surface_heat_celsius": gaussian(key_list[3], (LEAD_TIME_LENGTH, CATCHMENT_COUNT), 4.0, 12.0, ((1, 32),), jnp.float32),
        "potential_evapotranspiration": jnp.clip(0.01 * jax.random.uniform(key_list[4], (LEAD_TIME_LENGTH, CATCHMENT_COUNT), jnp.float32) ** block_levels(key_list[4], (LEAD_TIME_LENGTH, CATCHMENT_COUNT), ((1, 32),), -0.2, 0.2), 0.0, 0.01),
        "gauge_measured_values": jnp.clip(1.0 * jax.random.uniform(key_list[5], (BLOCKS, OBS), jnp.float32) ** block_levels(key_list[5], (BLOCKS, OBS), ((0, 32),), -0.2, 0.2), 0.0, 1.0),
        "gauge_deviation_sigma": jnp.clip(jnp.exp(math.log(0.5) - 2.3025851 * jax.random.uniform(key_list[6], (BLOCKS, OBS), jnp.float32) ** block_levels(key_list[6], (BLOCKS, OBS), ((0, 32),), -0.2, 0.2)), 0.05, 0.5),
        "gauge_perturbation_draws": gaussian(key_list[7], (BLOCKS, OBS, ENSEMBLE_SIZE), 1.0, 6.0, ((0, 32), (2, 16)), jnp.float32),
        "gauge_catchment_position": plant(jax.random.randint(key_list[8], (BLOCKS, OBS), 0, NB), jax.random.fold_in(key_list[8], 1), 0, NB - 1).astype(jnp.int32),
        "gauge_present_flag": plant((jax.random.randint(key_list[9], (BLOCKS, OBS), 0, 4) < 3).astype(jnp.int32), jax.random.fold_in(key_list[9], 1), 0, 1),
        "adjacent_block_list": draw_adjacent_block_list(jax.random.fold_in(key_list[11], 71), 0),
    }


PARAM_LOW = (-1.5, 0.0002, 0.8, 1.0, 0.4, 0.01, 0.002, 0.0001, 0.1, 0.0001)
PARAM_HIGH = (1.5, 0.002, 4.0, 5.0, 1.0, 0.05, 0.02, 0.002, 0.5, 0.001)

def unpack_params(normalized_catchment_settings):
    return tuple((PARAM_LOW[k] + (PARAM_HIGH[k] - PARAM_LOW[k]) * normalized_catchment_settings[k] for k in range(10)))

def hbv_hour(reservoir_contents, forcing, hydrologic_settings):
    snowpack, moisture, upper_zone, lower_zone = reservoir_contents
    rain_in, air_temp, evap_pot = forcing
    thresh, melt_rate, field_cap, shape_exp, evap_limit, quick_rate, upper_rate, lower_rate, upper_limit, percolation = hydrologic_settings
    snow_share = jnp.clip((thresh + 1.0 - air_temp) * 0.5, 0.0, 1.0)
    snowpack = snowpack + snow_share * rain_in
    snowmelt = jnp.minimum(melt_rate * jnp.maximum(air_temp - thresh, 0.0), snowpack)
    snowpack = snowpack - snowmelt
    inflow = (1.0 - snow_share) * rain_in + snowmelt
    recharge = inflow * jnp.power(moisture / field_cap, shape_exp)
    moisture = moisture + inflow - recharge
    excess = jnp.maximum(moisture - field_cap, 0.0)
    moisture = moisture - excess
    actual = jnp.minimum(evap_pot * jnp.minimum(moisture / (evap_limit * field_cap), 1.0), moisture)
    moisture = moisture - actual
    upper_zone = upper_zone + recharge + excess
    perc_flow = jnp.minimum(percolation, upper_zone)
    upper_zone = upper_zone - perc_flow
    lower_zone = lower_zone + perc_flow
    quick_flow = quick_rate * jnp.maximum(upper_zone - upper_limit, 0.0)
    slow_flow = upper_rate * upper_zone
    base_flow = lower_rate * lower_zone
    upper_zone = upper_zone - quick_flow - slow_flow
    lower_zone = lower_zone - base_flow
    return ((snowpack, moisture, upper_zone, lower_zone), quick_flow + slow_flow + base_flow)

def predict_ensemble_discharge(initial_reservoir_levels, normalized_catchment_settings, rainfall_member_series, surface_heat_celsius, potential_evapotranspiration):
    hydrologic_settings = unpack_params(normalized_catchment_settings)
    reservoir_contents = (initial_reservoir_levels[:, 0], initial_reservoir_levels[:, 1], initial_reservoir_levels[:, 2], initial_reservoir_levels[:, 3])

    def advance_single_interval(carry, forcing):
        new_state, runoff = hbv_hour(carry, forcing, hydrologic_settings)
        return (new_state, 100.0 * runoff)
    reservoir_contents, discharge_series = lax.scan(advance_single_interval, reservoir_contents, (rainfall_member_series, surface_heat_celsius, potential_evapotranspiration))
    return (reservoir_contents, discharge_series, hydrologic_settings)

def reference(initial_reservoir_levels, normalized_catchment_settings, rainfall_member_series, surface_heat_celsius, potential_evapotranspiration, gauge_measured_values, gauge_deviation_sigma, gauge_perturbation_draws, gauge_catchment_position, gauge_present_flag, adjacent_block_list):
    highest = lax.Precision.HIGHEST
    reservoir_contents, discharge_series, hydrologic_settings = predict_ensemble_discharge(initial_reservoir_levels, normalized_catchment_settings, rainfall_member_series, surface_heat_celsius, potential_evapotranspiration)
    snowpack, moisture, upper_zone, lower_zone = reservoir_contents
    members = moisture.shape[0]
    blocks = gauge_measured_values.shape[0]
    wetness = 0.45 * moisture / hydrologic_settings[2]
    slot_gauge = jnp.arange(OBS) < OBS // 2

    def pick(field):
        grid = field.reshape(members, blocks, NB)
        return jnp.take_along_axis(grid, gauge_catchment_position[None], axis=2)
    predicted = jnp.where(slot_gauge, pick(discharge_series[-1]), pick(wetness))
    predicted = jnp.transpose(predicted, (1, 2, 0))
    perturbed = gauge_measured_values[..., None] + gauge_deviation_sigma[..., None] * gauge_perturbation_draws
    avail = gauge_present_flag.astype(jnp.float32)

    def localize(table):
        joined = jnp.concatenate([table[:, None], table[adjacent_block_list]], axis=1)
        return joined.reshape((blocks, LOCAL) + table.shape[2:])
    local_pred = localize(predicted)
    local_pert = localize(perturbed)
    local_sd = localize(gauge_deviation_sigma)
    local_avail = localize(avail)
    anomaly = local_avail[..., None] * (local_pred - jnp.mean(local_pred, axis=2, keepdims=True))
    innovation = local_avail[..., None] * (local_pert - local_pred)
    state_rows = jnp.concatenate([moisture.reshape(members, blocks, NB), upper_zone.reshape(members, blocks, NB)], axis=2)
    state_rows = jnp.transpose(state_rows, (1, 2, 0))
    state_anom = state_rows - jnp.mean(state_rows, axis=2, keepdims=True)
    scale = 1.0 / (members - 1)
    obs_cov = jnp.einsum('blm,bkm->blk', anomaly, anomaly, precision=highest) * scale
    obs_cov = obs_cov + local_sd[:, :, None] ** 2 * jnp.eye(LOCAL, dtype=jnp.float32)
    cross = jnp.einsum('brm,blm->brl', state_anom, anomaly, precision=highest) * scale
    factor = jnp.linalg.cholesky(obs_cov)
    weights = jax.vmap(lambda lower_tri, rhs: jax.scipy.linalg.cho_solve((lower_tri, True), rhs))(factor, innovation)
    updated = state_rows + jnp.einsum('brl,blm->brm', cross, weights, precision=highest)
    updated = jnp.transpose(updated, (2, 0, 1))
    moisture_new = updated[..., :NB].reshape(members, -1)
    upper_new = updated[..., NB:].reshape(members, -1)
    analysis = jnp.stack([snowpack, moisture_new, upper_new, lower_zone], axis=1)
    return (analysis, discharge_series)
```

```python
import functools
import math

import jax
import jax.numpy as jnp
from jax import lax
from jax.experimental import pallas as pl
from jax.experimental.pallas import tpu as pltpu
from jax.sharding import PartitionSpec as P

f32 = jnp.float32
NB = 256
OBS = 32
NBR = 3
BLK = 4
HOURS = 24
MEM = 4
NBAS = 32
NMEM = 16
MESH = pl.DeviceIdType.MESH
HIGHEST = lax.Precision.HIGHEST
NT = (((1,), (1,)), ((), ()))
LOG2E = math.log2(math.e)

PARAM_LOW = (-1.5, 0.0002, 0.8, 1.0, 0.4, 0.01, 0.002, 0.0001, 0.1, 0.0001)
PARAM_HIGH = (1.5, 0.002, 4.0, 5.0, 1.0, 0.05, 0.02, 0.002, 0.5, 0.001)


def hour_step(states, rains, temp, evap, par):
    (thresh, melt_rate, field_cap, inv_cap, shape_log, inv_limit,
     quick_rate, upper_rate, lower_rate, upper_limit, percolation) = par
    share = jnp.clip((thresh + 1.0 - temp) * 0.5, 0.0, 1.0)
    dry = 1.0 - share
    melt_cap = melt_rate * jnp.maximum(temp - thresh, 0.0)
    out = []
    flows = []
    for (snow, moist, upper, lower), rain in zip(states, rains):
        snow = snow + share * rain
        melt = jnp.minimum(melt_cap, snow)
        snow = snow - melt
        inflow = dry * rain + melt
        recharge = inflow * jnp.exp2(shape_log * jnp.log(moist * inv_cap))
        moist = moist + inflow - recharge
        excess = jnp.maximum(moist - field_cap, 0.0)
        moist = moist - excess
        actual = jnp.minimum(evap * jnp.minimum(moist * inv_limit, 1.0), moist)
        moist = moist - actual
        upper = upper + recharge + excess
        perc = jnp.minimum(percolation, upper)
        upper = upper - perc
        lower = lower + perc
        quick = quick_rate * jnp.maximum(upper - upper_limit, 0.0)
        slow = upper_rate * upper
        base = lower_rate * lower
        upper = upper - quick - slow
        lower = lower - base
        out.append((snow, moist, upper, lower))
        flows.append(100.0 * (quick + slow + base))
    return out, flows


def eliminate(blocks):
    blocks = [list(b) for b in blocks]
    shape = (8, 128)
    for k in range(0, 64, 2):
        kt, kr = divmod(k, 8)
        for b in blocks:
            r0 = jnp.broadcast_to(b[kt][kr:kr + 1, :], shape)
            r1 = jnp.broadcast_to(b[kt][kr + 1:kr + 2, :], shape)
            a = jnp.broadcast_to(r0[:, k:k + 1], shape)
            o = jnp.broadcast_to(r0[:, k + 1:k + 2], shape)
            d = jnp.broadcast_to(r1[:, k + 1:k + 2], shape)
            inv = 1.0 / (a * d - o * o)
            n0 = (d * r0 - o * r1) * inv
            n1 = (a * r1 - o * r0) * inv
            for t in range(kt, 9):
                c0 = jnp.broadcast_to(b[t][:, k:k + 1], shape)
                c1 = jnp.broadcast_to(b[t][:, k + 1:k + 2], shape)
                b[t] = b[t] - (c0 * n0 + c1 * n1)
    return [b[8] for b in blocks]


def kernel(init, prm, rain, temp, evap, meas, sig, draws, pos, flag, adj, an_out, q_out,
           init_v, prm_v, rain_v, temp_v, evap_v, meas_v, sig_v, draws_v, pos_v, flag_v,
           prow_v, q_v, an_v, oh_v, turn_v, gath, sz, xz,
           in_sem, out_sem, gs_sem, gr_sem, ss_sem, sr_sem, xs_sem, xr_sem):
    me_b = lax.axis_index("basin")
    me_z = lax.axis_index("member")
    shape = (8, 128)
    lane = lax.broadcasted_iota(jnp.int32, shape, 1)
    row = lax.broadcasted_iota(jnp.int32, shape, 0)
    top = row < 4

    def zmod(v):
        return lax.rem(v + 2 * NMEM, NMEM)

    barrier = pltpu.get_barrier_semaphore()

    def greet(d, carry):
        pl.semaphore_signal(barrier, inc=1, device_id={"basin": lax.rem(me_b + d, NBAS)}, device_id_type=MESH)
        return carry

    lax.fori_loop(1, NBAS, greet, 0)
    for d in (1, -1, 2, -2, 3, -3, 4, -4):
        pl.semaphore_signal(barrier, inc=1, device_id={"member": zmod(me_z + d)}, device_id_type=MESH)

    loads = []
    for src, dst in ((sig, sig_v), (flag, flag_v), (meas, meas_v), (draws, draws_v), (pos, pos_v),
                     (prm, prm_v), (temp, temp_v), (evap, evap_v), (init, init_v), (rain, rain_v)):
        cp = pltpu.make_async_copy(src, dst, in_sem.at[len(loads)])
        cp.start()
        loads.append(cp)
    for cp in loads[:5]:
        cp.wait()

    weights, perts, places = [], [], []
    for i in range(BLK):
        sd = sig_v[i:i + 1, :]
        weights.append(jnp.broadcast_to(flag_v[i:i + 1, :].astype(f32) / sd, (8, OBS)))
        pert = meas_v[i:i + 1, :] + sd * draws_v[i]
        perts.append(jnp.concatenate([pert, pert], axis=0))
        places.append(jnp.broadcast_to(pos_v[i:i + 1, :] + NB * i, (8, OBS)))
    weight = jnp.concatenate(weights, axis=1)
    pert = jnp.concatenate(perts, axis=1)
    place = jnp.concatenate(places, axis=1)
    place16 = jnp.concatenate([place, place], axis=0)
    row16 = lax.broadcasted_iota(jnp.int32, (16, 128), 0)
    for j in range(64):
        oh_v[16 * j:16 * j + 16, :] = jnp.where(place16 == row16 + 16 * j, 1.0, 0.0).astype(jnp.bfloat16)

    loads[5].wait()
    par = []
    for s in range(8):
        prow_v[8 * s:8 * s + 8, :] = prm_v[0:8, 128 * s:128 * s + 128]
        prow_v[64 + 2 * s:66 + 2 * s, :] = prm_v[8:10, 128 * s:128 * s + 128]
    for k in range(10):
        v = prow_v[pl.ds(k, 8, stride=8), :] if k < 8 else prow_v[pl.ds(64 + k - 8, 8, stride=2), :]
        par.append(PARAM_LOW[k] + (PARAM_HIGH[k] - PARAM_LOW[k]) * v)
    tt, cfmax, fc, beta, lp, k0, k1, k2, uzl, perc = par
    inv_fc = 1.0 / fc
    hydro = (tt, cfmax, fc, inv_fc, beta * LOG2E, 1.0 / (lp * fc), k0, k1, k2, uzl, perc)

    for cp in loads[6:]:
        cp.wait()
    states = [tuple(init_v[pl.ds(32 * m + c, 8, stride=4), :] for c in range(4)) for m in range(MEM)]

    def eight_hours(chunk, states):
        flows = None
        for h in range(8):
            base = chunk * 256 + 32 * h
            rains = [rain_v[pl.ds(base + m, 8, stride=4), :] for m in range(MEM)]
            tmp = temp_v[pl.ds(chunk * 64 + h, 8, stride=8), :]
            eva = evap_v[pl.ds(chunk * 64 + h, 8, stride=8), :]
            states, flows = hour_step(states, rains, tmp, eva, hydro)
            for m in range(MEM):
                q_v[pl.ds(base + m, 8, stride=4), :] = flows[m]
        return states, flows

    states, flows = lax.fori_loop(
        0, 3, lambda c, s: eight_hours(c, s[0]),
        (states, [jnp.zeros(shape, f32)] * MEM))
    q_copy = pltpu.make_async_copy(q_v, q_out, out_sem.at[0])
    q_copy.start()

    for m in range(MEM):
        turn_v[8 * m:8 * m + 8, :] = states[m][1]
        turn_v[32 + 8 * m:40 + 8 * m, :] = states[m][2]
    for s in range(8):
        xz[0, 8 * s:8 * s + 8, :] = turn_v[pl.ds(s, 8, stride=8), :]
    for m in range(MEM):
        turn_v[64 + 8 * m:72 + 8 * m, :] = flows[m]
        turn_v[96 + 8 * m:104 + 8 * m, :] = 0.45 * states[m][1] * inv_fc
    field = jnp.concatenate([turn_v[pl.ds(64 + s, 8, stride=8), :] for s in range(8)], axis=1)
    hi = field.astype(jnp.bfloat16).astype(f32)
    mid = (field - hi).astype(jnp.bfloat16).astype(f32)
    low = field - hi - mid
    stack = jnp.concatenate([hi, mid, low, jnp.zeros_like(low)], axis=0).astype(jnp.bfloat16)
    picked = jnp.dot(stack, oh_v[...], preferred_element_type=f32)
    both = picked[0:8] + picked[8:16] + picked[16:24]
    swapped = pltpu.roll(both, 4, 0)
    pred = jnp.where(top == (lax.rem(lane, OBS) < OBS // 2), both, swapped)
    tile = weight * jnp.where(top, pred, pert - pred)
    gath[31] = tile

    pl.semaphore_wait(barrier, NBAS - 1 + 8)

    def x_copy(slot):
        if slot <= 8:
            src, to = slot - 1, 1
        else:
            src, to = (slot + 1) % NMEM, -1
        return pltpu.make_async_remote_copy(
            xz.at[src], xz.at[slot], xs_sem.at[slot - 1], xr_sem.at[slot - 1],
            device_id={"member": zmod(me_z + to)}, device_id_type=MESH)

    def g_copy(d):
        return pltpu.make_async_remote_copy(
            gath.at[31], gath.at[d - 1], gs_sem.at[d - 1], gr_sem.at[d - 1],
            device_id={"basin": lax.rem(me_b + d, NBAS)}, device_id_type=MESH)

    def s_copy(src, slot, to):
        return pltpu.make_async_remote_copy(
            sz.at[src], sz.at[slot], ss_sem.at[slot - 1], sr_sem.at[slot - 1],
            device_id={"member": zmod(me_z + to)}, device_id_type=MESH)

    def g_start(d, carry):
        g_copy(d).start()
        return carry

    lax.fori_loop(1, NBAS, g_start, 0)
    x_copy(1).start()
    x_copy(15).start()

    def x_next(step):
        x_copy(step).wait_recv()
        x_copy(step + 1).start()
        if step < 7:
            x_copy(16 - step).wait_recv()
            x_copy(15 - step).start()

    x_next(1)
    x_next(2)

    def g_wait(d, carry):
        g_copy(d).wait_recv()
        return carry

    lax.fori_loop(1, NBAS, g_wait, 0)

    local = []
    for i in range(BLK):
        piece = tile if i == 0 else pltpu.roll(tile, 128 - OBS * i, 1)
        for j in range(NBR):
            n = adj[j, me_b * BLK + i]
            slot = lax.rem(me_b + 2 * NBAS - 1 - lax.div(n, BLK), NBAS)
            shift = lax.rem(OBS * (j + 1) + 128 - OBS * lax.rem(n, BLK), 128)
            far = pltpu.roll(gath[slot], shift, 1)
            piece = jnp.where(lax.div(lane, OBS) == j + 1, far, piece)
        local.append(piece)
    turned = [pltpu.roll(p, 4, 0) for p in local]
    for p in range(2):
        sz[0, 8 * p:8 * p + 8, :] = jnp.where(top, local[2 * p], turned[2 * p + 1])
    obs_side = [jnp.where(top, t, p) for t, p in zip(turned, local)]

    for d in (4, 3, 2, 1):
        s_copy(0, d, d).start()
        s_copy(0, NMEM - d, -d).start()

    x_next(3)
    x_next(4)
    s_copy(0, 4, 4).wait_recv()
    for d in (4, 3, 2, 1):
        s_copy(4, 4 + d, d).start()
    s_copy(0, 12, -4).wait_recv()
    for d in (3, 2, 1):
        s_copy(12, 12 - d, -d).start()
    x_next(5)
    x_next(6)
    x_next(7)
    for slot in (1, 2, 3, 13, 14, 15):
        s_copy(0, slot, 1).wait_recv()
    for slot in (5, 6, 7, 8, 9, 10, 11):
        s_copy(0, slot, 1).wait_recv()

    systems = []
    big_row = lax.broadcasted_iota(jnp.int32, (72, 128), 0)
    big_lane = lax.broadcasted_iota(jnp.int32, (72, 128), 1)
    unit = jnp.where((big_row < 64) & ((big_lane == big_row) | (big_lane == big_row + 64)), 1.0, 0.0)
    for i in range(BLK):
        p, odd = divmod(i, 2)
        tiles = []
        for q in range(8):
            a = sz[q, 8 * p:8 * p + 8, :]
            b = sz[q + 8, 8 * p:8 * p + 8, :]
            if odd:
                tiles.append(jnp.where(top, pltpu.roll(a, 4, 0), b))
            else:
                tiles.append(jnp.where(top, a, pltpu.roll(b, 4, 0)))
        total = functools.reduce(jnp.add, tiles)
        mean = jnp.sum(total, axis=0, keepdims=True) * (1.0 / 64.0)
        centred = jnp.concatenate(tiles, axis=0) - mean
        left = jnp.concatenate([centred, obs_side[i]], axis=0)
        right = jnp.concatenate([centred, jnp.zeros_like(centred)], axis=0)
        gram = lax.dot_general(left, right, NT, precision=HIGHEST, preferred_element_type=f32)
        system = gram * (1.0 / 63.0) + unit
        systems.append([system[8 * t:8 * t + 8] for t in range(9)])
    solved = eliminate(systems)

    x_copy(8).wait_recv()
    x_copy(9).wait_recv()

    keep = top == (lax.rem(lane, 8) < 4)
    for i in range(BLK):
        t = jnp.where(lane >= 64, -solved[i], 0.0)
        t = t - jnp.sum(t, axis=1, keepdims=True) * (1.0 / 64.0)
        coef = jnp.where(
            lane >= 64,
            jnp.where(top, pltpu.roll(t, 124, 1), t),
            jnp.where(top, pltpu.roll(t, 64, 1), pltpu.roll(t, 68, 1)))
        coef = jnp.where(keep, coef, 0.0)
        for s in (2 * i, 2 * i + 1):
            stored = xz[:, 8 * s:8 * s + 8, :].reshape(128, 128)
            new = xz[0, 8 * s:8 * s + 8, :] + jnp.dot(
                coef, stored, precision=HIGHEST, preferred_element_type=f32)
            an_v[pl.ds(4 * s + 1, 4, stride=32), :] = new[0:4]
            an_v[pl.ds(4 * s + 2, 4, stride=32), :] = new[4:8]
    for m in range(MEM):
        an_v[pl.ds(32 * m, 8, stride=4), :] = states[m][0]
        an_v[pl.ds(32 * m + 3, 8, stride=4), :] = states[m][3]
    an_copy = pltpu.make_async_copy(an_v, an_out, out_sem.at[1])
    an_copy.start()

    def g_done(d, carry):
        g_copy(d).wait_send()
        return carry

    lax.fori_loop(1, NBAS, g_done, 0)
    for slot in range(1, NMEM):
        s_copy(0, slot, 1).wait_send()
        x_copy(slot).wait_send()
    q_copy.wait()
    an_copy.wait()


def on_device(init, prm, rain, temp, evap, meas, sig, draws, pos, flag, adj):
    def member_rows(a):
        return a.reshape(-1, 4, 8, 128).transpose(0, 2, 1, 3).reshape(-1, 128)

    def hour_rows(a):
        return a.reshape(3, 8, 8, 128).transpose(0, 2, 1, 3).reshape(192, 128)

    any_spec = pl.BlockSpec(memory_space=pl.ANY)
    dma = pltpu.SemaphoreType.DMA
    an, q = pl.pallas_call(
        kernel,
        out_shape=(jax.ShapeDtypeStruct((128, 128), f32), jax.ShapeDtypeStruct((768, 128), f32)),
        in_specs=[any_spec] * 10 + [pl.BlockSpec(memory_space=pltpu.SMEM)],
        out_specs=(any_spec, any_spec),
        scratch_shapes=[
            pltpu.VMEM((128, 128), f32), pltpu.VMEM((10, 1024), f32), pltpu.VMEM((768, 128), f32),
            pltpu.VMEM((192, 128), f32), pltpu.VMEM((192, 128), f32),
            pltpu.VMEM((4, 32), f32), pltpu.VMEM((4, 32), f32), pltpu.VMEM((4, 4, 32), f32),
            pltpu.VMEM((4, 32), jnp.int32), pltpu.VMEM((4, 32), jnp.int32),
            pltpu.VMEM((80, 128), f32), pltpu.VMEM((768, 128), f32), pltpu.VMEM((128, 128), f32),
            pltpu.VMEM((1024, 128), jnp.bfloat16), pltpu.VMEM((128, 128), f32),
            pltpu.VMEM((32, 8, 128), f32), pltpu.VMEM((16, 16, 128), f32), pltpu.VMEM((16, 64, 128), f32),
            dma((10,)), dma((2,)), dma((31,)), dma((31,)), dma((15,)), dma((15,)), dma((15,)), dma((15,)),
        ],
        compiler_params=pltpu.CompilerParams(collective_id=0, has_side_effects=True),
    )(member_rows(init), prm, member_rows(rain), hour_rows(temp), hour_rows(evap), meas, sig,
      draws.transpose(0, 2, 1), pos, flag, adj.T)

    def whole(a):
        return a.reshape(-1, 8, 4, 128).transpose(0, 2, 1, 3).reshape(-1, 4, 1024)

    return whole(an), whole(q)


def solution(mesh):
    placed = (
        P("member", None, "basin"),
        P(None, "basin"),
        P(None, "member", "basin"),
        P(None, "basin"),
        P(None, "basin"),
        P("basin", None),
        P("basin", None),
        P("basin", None, "member"),
        P("basin", None),
        P("basin", None),
        P(),
    )
    return jax.shard_map(
        on_device,
        mesh=mesh,
        in_specs=placed,
        out_specs=(P("member", None, "basin"), P(None, "member", "basin")),
        check_vma=False,
    )
```

```python
import functools
import math

import jax
import jax.numpy as jnp
from jax import lax
from jax.experimental import pallas as pl
from jax.experimental.pallas import tpu as pltpu
from jax.sharding import PartitionSpec as P

f32 = jnp.float32
NB = 256
OBS = 32
NBR = 3
BLK = 4
HOURS = 24
MEM = 4
NBAS = 32
NMEM = 16
X_REACH = 3
S_REACH = 4
REACH = 4
XLATE = 1
LIMIT = 16 * 1024 * 1024

MESH = pl.DeviceIdType.MESH
HIGHEST = lax.Precision.HIGHEST
NT = (((1,), (1,)), ((), ()))
LOG2E = math.log2(math.e)

PARAM_LOW = (-1.5, 0.0002, 0.8, 1.0, 0.4, 0.01, 0.002, 0.0001, 0.1, 0.0001)
PARAM_HIGH = (1.5, 0.002, 4.0, 5.0, 1.0, 0.05, 0.02, 0.002, 0.5, 0.001)


def hour_step(states, rains, temp, evap, par):
    (thresh, melt_rate, field_cap, inv_cap, shape_log, inv_limit,
     quick_rate, upper_rate, lower_rate, upper_limit, percolation) = par
    share = jnp.clip((thresh + 1.0 - temp) * 0.5, 0.0, 1.0)
    dry = 1.0 - share
    melt_cap = melt_rate * jnp.maximum(temp - thresh, 0.0)
    out = []
    flows = []
    for (snow, moist, upper, lower), rain in zip(states, rains):
        snow = snow + share * rain
        melt = jnp.minimum(melt_cap, snow)
        snow = snow - melt
        inflow = dry * rain + melt
        recharge = inflow * jnp.exp2(shape_log * jnp.log(moist * inv_cap))
        moist = moist + inflow - recharge
        excess = jnp.maximum(moist - field_cap, 0.0)
        moist = moist - excess
        actual = jnp.minimum(evap * jnp.minimum(moist * inv_limit, 1.0), moist)
        moist = moist - actual
        upper = upper + recharge + excess
        perc = jnp.minimum(percolation, upper)
        upper = upper - perc
        lower = lower + perc
        quick = quick_rate * jnp.maximum(upper - upper_limit, 0.0)
        slow = upper_rate * upper
        base = lower_rate * lower
        upper = upper - quick - slow
        lower = lower - base
        out.append((snow, moist, upper, lower))
        flows.append(100.0 * (quick + slow + base))
    return out, flows


def eliminate(blocks):
    blocks = [list(b) for b in blocks]
    shape = (8, 128)

    def wide(v, k):
        return jnp.broadcast_to(v[:, k:k + 1], shape)

    for k in range(0, 64, 4):
        kt, kr = divmod(k, 8)
        for b in blocks:
            r = [jnp.broadcast_to(b[kt][kr + j:kr + j + 1, :], shape) for j in range(4)]
            a00, a01, b00, b01 = (wide(r[0], k + j) for j in range(4))
            a11, b10, b11 = (wide(r[1], k + j) for j in (1, 2, 3))
            d00, d01 = (wide(r[2], k + j) for j in (2, 3))
            d11 = wide(r[3], k + 3)
            inv = 1.0 / (a00 * a11 - a01 * a01)
            i00, i01, i11 = a11 * inv, -a01 * inv, a00 * inv
            g00, g01 = i00 * b00 + i01 * b10, i00 * b01 + i01 * b11
            g10, g11 = i01 * b00 + i11 * b10, i01 * b01 + i11 * b11
            s00 = d00 - (b00 * g00 + b10 * g10)
            s01 = d01 - (b00 * g01 + b10 * g11)
            s11 = d11 - (b01 * g01 + b11 * g11)
            jnv = 1.0 / (s00 * s11 - s01 * s01)
            q2 = r[2] - (g00 * r[0] + g10 * r[1])
            q3 = r[3] - (g01 * r[0] + g11 * r[1])
            n2 = (s11 * q2 - s01 * q3) * jnv
            n3 = (s00 * q3 - s01 * q2) * jnv
            n0 = i00 * r[0] + i01 * r[1] - (g00 * n2 + g01 * n3)
            n1 = i01 * r[0] + i11 * r[1] - (g10 * n2 + g11 * n3)
            for t in range(kt + kr // 4, 9):
                c = [wide(b[t], k + j) for j in range(4)]
                b[t] = b[t] - ((c[0] * n0 + c[1] * n1) + (c[2] * n2 + c[3] * n3))
    return [b[8] for b in blocks]


def kernel(init, prm, rain, temp, evap, meas, sig, draws, pos, flag, adj_hbm, an_v, q_v,
           init_v, prm_v, rain_v, temp_v, evap_v, meas_v, sig_v, draws_v, pos_v, flag_v, adj,
           prow_v, oh_v, turn_v, gath, sz, xz,
           in_sem, gs_sem, gr_sem, ss_sem, sr_sem, xs_sem, xr_sem):
    me_b = lax.axis_index("basin")
    me_z = lax.axis_index("member")
    shape = (8, 128)
    lane = lax.broadcasted_iota(jnp.int32, shape, 1)
    row = lax.broadcasted_iota(jnp.int32, shape, 0)
    top = row < 4

    def zmod(v):
        return lax.rem(v + 2 * NMEM, NMEM)

    barrier = pltpu.get_barrier_semaphore()

    def greet(d, carry):
        pl.semaphore_signal(barrier, inc=1, device_id={"basin": lax.rem(me_b + d, NBAS)}, device_id_type=MESH)
        return carry

    lax.fori_loop(1, NBAS, greet, 0)
    for d in range(1, REACH + 1):
        for to in {d, NMEM - d}:
            pl.semaphore_signal(barrier, inc=1, device_id={"member": zmod(me_z + to)}, device_id_type=MESH)

    loads = []
    for src, dst in ((sig, sig_v), (flag, flag_v), (meas, meas_v), (draws, draws_v), (pos, pos_v),
                     (prm, prm_v), (temp, temp_v), (evap, evap_v), (init, init_v), (rain, rain_v), (adj_hbm, adj)):
        cp = pltpu.make_async_copy(src, dst, in_sem.at[len(loads)])
        cp.start()
        loads.append(cp)
    for cp in loads[:5]:
        cp.wait()

    weights, perts, places = [], [], []
    for i in range(BLK):
        sd = sig_v[i:i + 1, :]
        weights.append(jnp.broadcast_to(flag_v[i:i + 1, :].astype(f32) / sd, (8, OBS)))
        pert = meas_v[i:i + 1, :] + sd * draws_v[i]
        perts.append(jnp.concatenate([pert, pert], axis=0))
        places.append(jnp.broadcast_to(pos_v[i:i + 1, :] + NB * i, (8, OBS)))
    weight = jnp.concatenate(weights, axis=1)
    pert = jnp.concatenate(perts, axis=1)
    place = jnp.concatenate(places, axis=1)
    place16 = jnp.concatenate([place, place], axis=0)
    row16 = lax.broadcasted_iota(jnp.int32, (16, 128), 0)
    for j in range(64):
        oh_v[16 * j:16 * j + 16, :] = jnp.where(place16 == row16 + 16 * j, 1.0, 0.0).astype(jnp.bfloat16)

    loads[5].wait()
    par = []
    for s in range(8):
        prow_v[8 * s:8 * s + 8, :] = prm_v[0:8, 128 * s:128 * s + 128]
        prow_v[64 + 2 * s:66 + 2 * s, :] = prm_v[8:10, 128 * s:128 * s + 128]
    for k in range(10):
        v = prow_v[pl.ds(k, 8, stride=8), :] if k < 8 else prow_v[pl.ds(64 + k - 8, 8, stride=2), :]
        par.append(PARAM_LOW[k] + (PARAM_HIGH[k] - PARAM_LOW[k]) * v)
    tt, cfmax, fc, beta, lp, k0, k1, k2, uzl, perc = par
    inv_fc = 1.0 / fc
    hydro = (tt, cfmax, fc, inv_fc, beta * LOG2E, 1.0 / (lp * fc), k0, k1, k2, uzl, perc)

    for cp in loads[6:]:
        cp.wait()
    states = [tuple(init_v[pl.ds(32 * m + c, 8, stride=4), :] for c in range(4)) for m in range(MEM)]

    def eight_hours(chunk, states):
        flows = None
        for h in range(8):
            base = chunk * 256 + 32 * h
            rains = [rain_v[pl.ds(base + m, 8, stride=4), :] for m in range(MEM)]
            tmp = temp_v[pl.ds(chunk * 64 + h, 8, stride=8), :]
            eva = evap_v[pl.ds(chunk * 64 + h, 8, stride=8), :]
            states, flows = hour_step(states, rains, tmp, eva, hydro)
            for m in range(MEM):
                q_v[pl.ds(base + m, 8, stride=4), :] = flows[m]
        return states, flows

    states, flows = lax.fori_loop(
        0, 3, lambda c, s: eight_hours(c, s[0]),
        (states, [jnp.zeros(shape, f32)] * MEM))

    for m in range(MEM):
        turn_v[8 * m:8 * m + 8, :] = states[m][1]
        turn_v[32 + 8 * m:40 + 8 * m, :] = states[m][2]
    for s in range(8):
        xz[0, 8 * s:8 * s + 8, :] = turn_v[pl.ds(s, 8, stride=8), :]
    for m in range(MEM):
        turn_v[64 + 8 * m:72 + 8 * m, :] = flows[m]
        turn_v[96 + 8 * m:104 + 8 * m, :] = 0.45 * states[m][1] * inv_fc
    field = jnp.concatenate([turn_v[pl.ds(64 + s, 8, stride=8), :] for s in range(8)], axis=1)
    hi = field.astype(jnp.bfloat16).astype(f32)
    mid = (field - hi).astype(jnp.bfloat16).astype(f32)
    low = field - hi - mid
    stack = jnp.concatenate([hi, mid, low, jnp.zeros_like(low)], axis=0).astype(jnp.bfloat16)
    picked = jnp.dot(stack, oh_v[...], preferred_element_type=f32)
    both = picked[0:8] + picked[8:16] + picked[16:24]
    swapped = pltpu.roll(both, 4, 0)
    pred = jnp.where(top == (lax.rem(lane, OBS) < OBS // 2), both, swapped)
    tile = weight * jnp.where(top, pred, pert - pred)
    gath[31] = tile

    pl.semaphore_wait(barrier, NBAS - 1 + min(2 * REACH, NMEM - 1))

    def z_copy(buf, send, recv, src, slot, to):
        return pltpu.make_async_remote_copy(
            buf.at[src], buf.at[slot], send.at[slot - 1], recv.at[slot - 1],
            device_id={"member": zmod(me_z + to)}, device_id_type=MESH)

    def x_copy(src, slot, to):
        return z_copy(xz, xs_sem, xr_sem, src, slot, to)

    def s_copy(src, slot, to):
        return z_copy(sz, ss_sem, sr_sem, src, slot, to)

    def spread(copy, reach, base):
        if base:
            copy(0, base, 1).wait_recv()
            copy(0, NMEM - base, 1).wait_recv()
        for d in range(min(reach, 8 - base), 0, -1):
            copy(base, base + d, d).start()
            if base + d < 8:
                copy((NMEM - base) % NMEM, NMEM - base - d, -d).start()

    def settle(copy, reach):
        for slot in range(1, NMEM):
            hop = min(slot, NMEM - slot)
            if hop % reach or hop == 8:
                copy(0, slot, 1).wait_recv()

    def g_copy(d):
        return pltpu.make_async_remote_copy(
            gath.at[31], gath.at[d - 1], gs_sem.at[d - 1], gr_sem.at[d - 1],
            device_id={"basin": lax.rem(me_b + d, NBAS)}, device_id_type=MESH)

    for d in range(1, NBAS):
        g_copy(d).start()
    spread(x_copy, X_REACH, 0)
    for d in range(1, NBAS):
        g_copy(d).wait_recv()

    local = []
    for i in range(BLK):
        piece = tile if i == 0 else pltpu.roll(tile, 128 - OBS * i, 1)
        for j in range(NBR):
            n = adj[j, me_b * BLK + i]
            slot = lax.rem(me_b + 2 * NBAS - 1 - lax.div(n, BLK), NBAS)
            shift = lax.rem(OBS * (j + 1) + 128 - OBS * lax.rem(n, BLK), 128)
            far = pltpu.roll(gath[slot], shift, 1)
            piece = jnp.where(lax.div(lane, OBS) == j + 1, far, piece)
        local.append(piece)
    turned = [pltpu.roll(p, 4, 0) for p in local]
    for p in range(2):
        sz[0, 8 * p:8 * p + 8, :] = jnp.where(top, local[2 * p], turned[2 * p + 1])
    obs_side = [jnp.where(top, t, p) for t, p in zip(turned, local)]

    spread(s_copy, S_REACH, 0)
    bases = list(range(X_REACH, 8, X_REACH))
    for base in bases[:len(bases) - XLATE]:
        spread(x_copy, X_REACH, base)
    for base in range(S_REACH, 8, S_REACH):
        spread(s_copy, S_REACH, base)
    settle(s_copy, S_REACH)
    for base in bases[len(bases) - XLATE:]:
        spread(x_copy, X_REACH, base)

    systems = []
    big_row = lax.broadcasted_iota(jnp.int32, (72, 128), 0)
    big_lane = lax.broadcasted_iota(jnp.int32, (72, 128), 1)
    unit = jnp.where((big_row < 64) & ((big_lane == big_row) | (big_lane == big_row + 64)), 1.0, 0.0)
    for i in range(BLK):
        p, odd = divmod(i, 2)
        tiles = []
        for q in range(8):
            a = sz[q, 8 * p:8 * p + 8, :]
            b = sz[q + 8, 8 * p:8 * p + 8, :]
            if odd:
                tiles.append(jnp.where(top, pltpu.roll(a, 4, 0), b))
            else:
                tiles.append(jnp.where(top, a, pltpu.roll(b, 4, 0)))
        total = functools.reduce(jnp.add, tiles)
        mean = jnp.sum(total, axis=0, keepdims=True) * (1.0 / 64.0)
        centred = jnp.concatenate(tiles, axis=0) - mean
        left = jnp.concatenate([centred, obs_side[i]], axis=0)
        right = jnp.concatenate([centred, jnp.zeros_like(centred)], axis=0)
        gram = lax.dot_general(left, right, NT, precision=HIGHEST, preferred_element_type=f32)
        system = gram * (1.0 / 63.0) + unit
        systems.append([system[8 * t:8 * t + 8] for t in range(9)])
    solved = eliminate(systems)

    settle(x_copy, X_REACH)

    keep = top == (lax.rem(lane, 8) < 4)
    for i in range(BLK):
        t = jnp.where(lane >= 64, -solved[i], 0.0)
        t = t - jnp.sum(t, axis=1, keepdims=True) * (1.0 / 64.0)
        coef = jnp.where(
            lane >= 64,
            jnp.where(top, pltpu.roll(t, 124, 1), t),
            jnp.where(top, pltpu.roll(t, 64, 1), pltpu.roll(t, 68, 1)))
        coef = jnp.where(keep, coef, 0.0)
        for s in (2 * i, 2 * i + 1):
            stored = xz[:, 8 * s:8 * s + 8, :].reshape(128, 128)
            new = xz[0, 8 * s:8 * s + 8, :] + jnp.dot(
                coef, stored, precision=HIGHEST, preferred_element_type=f32)
            an_v[pl.ds(4 * s + 1, 4, stride=32), :] = new[0:4]
            an_v[pl.ds(4 * s + 2, 4, stride=32), :] = new[4:8]
    for m in range(MEM):
        an_v[pl.ds(32 * m, 8, stride=4), :] = states[m][0]
        an_v[pl.ds(32 * m + 3, 8, stride=4), :] = states[m][3]

    for d in range(1, NBAS):
        g_copy(d).wait_send()
    for slot in range(1, NMEM):
        s_copy(0, slot, 1).wait_send()
        x_copy(0, slot, 1).wait_send()


def hand_over(an, q, an_out, q_out, sem):
    copies = [pltpu.make_async_copy(q, q_out, sem.at[0]), pltpu.make_async_copy(an, an_out, sem.at[1])]
    for cp in copies:
        cp.start()
    for cp in copies:
        cp.wait()


def on_device(init, prm, rain, temp, evap, meas, sig, draws, pos, flag, adj):
    def member_rows(a):
        return a.reshape(-1, 4, 8, 128).transpose(0, 2, 1, 3).reshape(-1, 128)

    def hour_rows(a):
        return a.reshape(3, 8, 8, 128).transpose(0, 2, 1, 3).reshape(192, 128)

    any_spec = pl.BlockSpec(memory_space=pl.ANY)
    hbm_spec = pl.BlockSpec(memory_space=pltpu.HBM)
    dma = pltpu.SemaphoreType.DMA
    an, q = pl.pallas_call(
        kernel,
        out_shape=(jax.ShapeDtypeStruct((128, 128), f32), jax.ShapeDtypeStruct((768, 128), f32)),
        in_specs=[hbm_spec] * 11,
        out_specs=(pl.BlockSpec(memory_space=pltpu.VMEM),) * 2,
        scratch_shapes=[
            pltpu.VMEM((128, 128), f32), pltpu.VMEM((10, 1024), f32), pltpu.VMEM((768, 128), f32),
            pltpu.VMEM((192, 128), f32), pltpu.VMEM((192, 128), f32),
            pltpu.VMEM((4, 32), f32), pltpu.VMEM((4, 32), f32), pltpu.VMEM((4, 4, 32), f32),
            pltpu.VMEM((4, 32), jnp.int32), pltpu.VMEM((4, 32), jnp.int32), pltpu.SMEM((3, 128), jnp.int32),
            pltpu.VMEM((80, 128), f32),
            pltpu.VMEM((1024, 128), jnp.bfloat16), pltpu.VMEM((128, 128), f32),
            pltpu.VMEM((32, 8, 128), f32), pltpu.VMEM((16, 16, 128), f32), pltpu.VMEM((16, 64, 128), f32),
            dma((11,)), dma((31,)), dma((31,)), dma((15,)), dma((15,)), dma((15,)), dma((15,)),
        ],
        compiler_params=pltpu.CompilerParams(collective_id=0, has_side_effects=True, vmem_limit_bytes=LIMIT),
    )(*[pltpu.with_memory_space_constraint(a, pltpu.HBM) for a in (
        member_rows(init), prm, member_rows(rain), hour_rows(temp), hour_rows(evap), meas, sig,
        draws.transpose(0, 2, 1), pos, flag, adj.T)])

    an, q = pl.pallas_call(
        hand_over,
        out_shape=(jax.ShapeDtypeStruct((128, 128), f32), jax.ShapeDtypeStruct((768, 128), f32)),
        in_specs=[any_spec] * 2,
        out_specs=(any_spec, any_spec),
        scratch_shapes=[dma((2,))],
        compiler_params=pltpu.CompilerParams(vmem_limit_bytes=LIMIT),
    )(an, q)

    def whole(a):
        return a.reshape(-1, 8, 4, 128).transpose(0, 2, 1, 3).reshape(-1, 4, 1024)

    return whole(an), whole(q)


def solution(mesh):
    placed = (
        P("member", None, "basin"),
        P(None, "basin"),
        P(None, "member", "basin"),
        P(None, "basin"),
        P(None, "basin"),
        P("basin", None),
        P("basin", None),
        P("basin", None, "member"),
        P("basin", None),
        P("basin", None),
        P(),
    )
    return jax.shard_map(
        on_device,
        mesh=mesh,
        in_specs=placed,
        out_specs=(P("member", None, "basin"), P(None, "member", "basin")),
        check_vma=False,
    )
```

```python
import functools
import math

import jax
import jax.numpy as jnp
from jax import lax
from jax.experimental import pallas as pl
from jax.experimental.pallas import tpu as pltpu
from jax.sharding import PartitionSpec as P

f32 = jnp.float32
NB = 256
OBS = 32
NBR = 3
BLK = 4
HOURS = 24
MEM = 4
NBAS = 32
NMEM = 16
X_REACH = 3
S_REACH = 4
REACH = 4
ORDER = ('S0', 'X3', 'S4', 'W', 'X6')
LIMIT = 16 * 1024 * 1024

MESH = pl.DeviceIdType.MESH
HIGHEST = lax.Precision.HIGHEST
NT = (((1,), (1,)), ((), ()))
LOG2E = math.log2(math.e)

PARAM_LOW = (-1.5, 0.0002, 0.8, 1.0, 0.4, 0.01, 0.002, 0.0001, 0.1, 0.0001)
PARAM_HIGH = (1.5, 0.002, 4.0, 5.0, 1.0, 0.05, 0.02, 0.002, 0.5, 0.001)


STEPS = sorted(((dy, dx, dc) for dy in range(4) for dx in range(4) for dc in range(2)),
               key=lambda o: (-min(o[0], 4 - o[0]) - min(o[1], 4 - o[1]), -o[2]))[:-1]


def hour_step(states, rains, temp, evap, par):
    (thresh, melt_rate, field_cap, inv_cap, shape_log, inv_limit,
     quick_rate, upper_rate, lower_rate, upper_limit, percolation) = par
    share = jnp.clip((thresh + 1.0 - temp) * 0.5, 0.0, 1.0)
    dry = 1.0 - share
    melt_cap = melt_rate * jnp.maximum(temp - thresh, 0.0)
    out = []
    flows = []
    for (snow, moist, upper, lower), rain in zip(states, rains):
        snow = snow + share * rain
        melt = jnp.minimum(melt_cap, snow)
        snow = snow - melt
        inflow = dry * rain + melt
        recharge = inflow * jnp.exp2(shape_log * jnp.log(moist * inv_cap))
        moist = moist + inflow - recharge
        excess = jnp.maximum(moist - field_cap, 0.0)
        moist = moist - excess
        actual = jnp.minimum(evap * jnp.minimum(moist * inv_limit, 1.0), moist)
        moist = moist - actual
        upper = upper + recharge + excess
        perc = jnp.minimum(percolation, upper)
        upper = upper - perc
        lower = lower + perc
        quick = quick_rate * jnp.maximum(upper - upper_limit, 0.0)
        slow = upper_rate * upper
        base = lower_rate * lower
        upper = upper - quick - slow
        lower = lower - base
        out.append((snow, moist, upper, lower))
        flows.append(100.0 * (quick + slow + base))
    return out, flows


def eliminate(pairs):
    pairs = [list(b) for b in pairs]
    shape = (8, 128)
    lane = lax.broadcasted_iota(jnp.int32, shape, 1)
    half = lane - lane % 64

    def take(v, index, axis):
        return jnp.take_along_axis(v, index, axis=axis, mode="promise_in_bounds")

    for k in range(0, 64, 4):
        kt, kr = divmod(k, 8)
        here = [lane % 64 == k + j for j in range(4)]
        inside = (lane % 64 >= k) & (lane % 64 < k + 4)
        columns = [half + (k + j) for j in range(4)]
        for b in pairs:
            head = [take(b[kt], columns[j], 1) for j in range(4)]

            def at(i, j):
                return jnp.broadcast_to(head[j][kr + i:kr + i + 1, :], shape)

            r = [jnp.broadcast_to(b[kt][kr + j:kr + j + 1, :], shape) for j in range(4)]
            r = [jnp.where(inside, jnp.where(here[j], 1.0, 0.0), r[j]) for j in range(4)]
            a00, a01, b00, b01 = (at(0, j) for j in range(4))
            a11, b10, b11 = (at(1, j) for j in (1, 2, 3))
            d00, d01 = (at(2, j) for j in (2, 3))
            d11 = at(3, 3)
            inv = 1.0 / (a00 * a11 - a01 * a01)
            i00, i01, i11 = a11 * inv, -a01 * inv, a00 * inv
            g00, g01 = i00 * b00 + i01 * b10, i00 * b01 + i01 * b11
            g10, g11 = i01 * b00 + i11 * b10, i01 * b01 + i11 * b11
            s00 = d00 - (b00 * g00 + b10 * g10)
            s01 = d01 - (b00 * g01 + b10 * g11)
            s11 = d11 - (b01 * g01 + b11 * g11)
            jnv = 1.0 / (s00 * s11 - s01 * s01)
            q2 = r[2] - (g00 * r[0] + g10 * r[1])
            q3 = r[3] - (g01 * r[0] + g11 * r[1])
            n2 = (s11 * q2 - s01 * q3) * jnv
            n3 = (s00 * q3 - s01 * q2) * jnv
            n0 = i00 * r[0] + i01 * r[1] - (g00 * n2 + g01 * n3)
            n1 = i01 * r[0] + i11 * r[1] - (g10 * n2 + g11 * n3)
            for t in range(kt + kr // 4, 9):
                c = head if t == kt else [take(b[t], columns[j], 1) for j in range(4)]
                b[t] = jnp.where(inside, 0.0, b[t]) - ((c[0] * n0 + c[1] * n1) + (c[2] * n2 + c[3] * n3))
    return [b[8] for b in pairs]


def kernel(init, prm, rain, temp, evap, meas, sig, draws, pos, flag, adj_hbm, an_v, q_v,
           init_v, prm_v, rain_v, temp_v, evap_v, meas_v, sig_v, draws_v, pos_v, flag_v, adj,
           prow_v, oh_v, turn_v, gath, sz, xz,
           in_sem, gs_sem, gr_sem, ss_sem, sr_sem, xs_sem, xr_sem):
    me_b = lax.axis_index("basin")
    me_z = lax.axis_index("member")
    shape = (8, 128)
    lane = lax.broadcasted_iota(jnp.int32, shape, 1)
    row = lax.broadcasted_iota(jnp.int32, shape, 0)
    top = row < 4

    def zmod(v):
        return lax.rem(v + 2 * NMEM, NMEM)

    loads = []
    for src, dst in ((sig, sig_v), (flag, flag_v), (meas, meas_v), (draws, draws_v), (pos, pos_v),
                     (prm, prm_v), (temp, temp_v), (evap, evap_v), (init, init_v), (rain, rain_v), (adj_hbm, adj)):
        cp = pltpu.make_async_copy(src, dst, in_sem.at[len(loads)])
        cp.start()
        loads.append(cp)

    barrier = pltpu.get_barrier_semaphore()

    me_y, me_x, me_c = me_b // 8, (me_b // 2) % 4, me_b % 2

    def there(step):
        dy, dx, dc = step
        return {"basin": ((me_y + dy) % 4 * 4 + (me_x + dx) % 4) * 2 + (me_c + dc) % 2}

    for step in STEPS:
        pl.semaphore_signal(barrier, inc=1, device_id=there(step), device_id_type=MESH)
    for d in range(1, REACH + 1):
        for to in {d, NMEM - d}:
            pl.semaphore_signal(barrier, inc=1, device_id={"member": zmod(me_z + to)}, device_id_type=MESH)

    for cp in loads[:5]:
        cp.wait()

    weights, perts, places = [], [], []
    for i in range(BLK):
        sd = sig_v[i:i + 1, :]
        weights.append(jnp.broadcast_to(flag_v[i:i + 1, :].astype(f32) / sd, (8, OBS)))
        pert = meas_v[i:i + 1, :] + sd * draws_v[i]
        perts.append(jnp.concatenate([pert, pert], axis=0))
        places.append(jnp.broadcast_to(pos_v[i:i + 1, :] + NB * i, (8, OBS)))
    weight = jnp.concatenate(weights, axis=1)
    pert = jnp.concatenate(perts, axis=1)
    place = jnp.concatenate(places, axis=1)
    place16 = jnp.concatenate([place, place], axis=0)
    row16 = lax.broadcasted_iota(jnp.int32, (16, 128), 0)
    for j in range(64):
        oh_v[16 * j:16 * j + 16, :] = jnp.where(place16 == row16 + 16 * j, 1.0, 0.0).astype(jnp.bfloat16)

    loads[5].wait()
    par = []
    for s in range(8):
        prow_v[8 * s:8 * s + 8, :] = prm_v[0:8, 128 * s:128 * s + 128]
        prow_v[64 + 2 * s:66 + 2 * s, :] = prm_v[8:10, 128 * s:128 * s + 128]
    for k in range(10):
        v = prow_v[pl.ds(k, 8, stride=8), :] if k < 8 else prow_v[pl.ds(64 + k - 8, 8, stride=2), :]
        par.append(PARAM_LOW[k] + (PARAM_HIGH[k] - PARAM_LOW[k]) * v)
    tt, cfmax, fc, beta, lp, k0, k1, k2, uzl, perc = par
    inv_fc = 1.0 / fc
    hydro = (tt, cfmax, fc, inv_fc, beta * LOG2E, 1.0 / (lp * fc), k0, k1, k2, uzl, perc)

    for cp in loads[6:]:
        cp.wait()
    states = [tuple(init_v[pl.ds(32 * m + c, 8, stride=4), :] for c in range(4)) for m in range(MEM)]

    def eight_hours(chunk, states):
        flows = None
        for h in range(8):
            base = chunk * 256 + 32 * h
            rains = [rain_v[pl.ds(base + m, 8, stride=4), :] for m in range(MEM)]
            tmp = temp_v[pl.ds(chunk * 64 + h, 8, stride=8), :]
            eva = evap_v[pl.ds(chunk * 64 + h, 8, stride=8), :]
            states, flows = hour_step(states, rains, tmp, eva, hydro)
            for m in range(MEM):
                q_v[pl.ds(base + m, 8, stride=4), :] = flows[m]
        return states, flows

    states, flows = lax.fori_loop(
        0, 3, lambda c, s: eight_hours(c, s[0]),
        (states, [jnp.zeros(shape, f32)] * MEM))

    for m in range(MEM):
        turn_v[8 * m:8 * m + 8, :] = states[m][1]
        turn_v[32 + 8 * m:40 + 8 * m, :] = states[m][2]
    for s in range(8):
        xz[0, 8 * s:8 * s + 8, :] = turn_v[pl.ds(s, 8, stride=8), :]
    for m in range(MEM):
        turn_v[64 + 8 * m:72 + 8 * m, :] = flows[m]
        turn_v[96 + 8 * m:104 + 8 * m, :] = 0.45 * states[m][1] * inv_fc
    field = jnp.concatenate([turn_v[pl.ds(64 + s, 8, stride=8), :] for s in range(8)], axis=1)
    hi = field.astype(jnp.bfloat16).astype(f32)
    mid = (field - hi).astype(jnp.bfloat16).astype(f32)
    low = field - hi - mid
    stack = jnp.concatenate([hi, mid, low, jnp.zeros_like(low)], axis=0).astype(jnp.bfloat16)
    picked = jnp.dot(stack, oh_v[...], preferred_element_type=f32)
    both = picked[0:8] + picked[8:16] + picked[16:24]
    swapped = pltpu.roll(both, 4, 0)
    pred = jnp.where(top == (lax.rem(lane, OBS) < OBS // 2), both, swapped)
    tile = weight * jnp.where(top, pred, pert - pred)
    gath[0] = tile

    pl.semaphore_wait(barrier, NBAS - 1 + min(2 * REACH, NMEM - 1))

    def z_copy(buf, send, recv, src, slot, to):
        return pltpu.make_async_remote_copy(
            buf.at[src], buf.at[slot], send.at[slot - 1], recv.at[slot - 1],
            device_id={"member": zmod(me_z + to)}, device_id_type=MESH)

    def x_copy(src, slot, to):
        return z_copy(xz, xs_sem, xr_sem, src, slot, to)

    def s_copy(src, slot, to):
        return z_copy(sz, ss_sem, sr_sem, src, slot, to)

    def spread(copy, reach, base):
        if base:
            copy(0, base, 1).wait_recv()
            copy(0, NMEM - base, 1).wait_recv()
        for d in range(min(reach, 8 - base), 0, -1):
            copy(base, base + d, d).start()
            if base + d < 8:
                copy((NMEM - base) % NMEM, NMEM - base - d, -d).start()

    def settle(copy, reach):
        for slot in range(1, NMEM):
            hop = min(slot, NMEM - slot)
            if hop % reach or hop == 8:
                copy(0, slot, 1).wait_recv()

    def g_copy(step):
        slot = (step[0] * 4 + step[1]) * 2 + step[2]
        return pltpu.make_async_remote_copy(
            gath.at[0], gath.at[slot], gs_sem.at[slot - 1], gr_sem.at[slot - 1],
            device_id=there(step), device_id_type=MESH)

    for step in STEPS:
        g_copy(step).start()
    spread(x_copy, X_REACH, 0)
    for step in reversed(STEPS):
        g_copy(step).wait_recv()

    local = []
    for i in range(BLK):
        piece = tile if i == 0 else pltpu.roll(tile, 128 - OBS * i, 1)
        for j in range(NBR):
            n = adj[j, me_b * BLK + i]
            slot = ((me_y + 4 - n // 32) % 4 * 4 + (me_x + 4 - n // 8 % 4) % 4) * 2 + (me_c + 2 - n // 4 % 2) % 2
            shift = lax.rem(OBS * (j + 1) + 128 - OBS * lax.rem(n, BLK), 128)
            far = pltpu.roll(gath[slot], shift, 1)
            piece = jnp.where(lax.div(lane, OBS) == j + 1, far, piece)
        local.append(piece)
    turned = [pltpu.roll(p, 4, 0) for p in local]
    for p in range(2):
        sz[0, 8 * p:8 * p + 8, :] = jnp.where(top, local[2 * p], turned[2 * p + 1])
    obs_side = [jnp.where(top, t, p) for t, p in zip(turned, local)]

    for what in ORDER:
        if what == "W":
            settle(s_copy, S_REACH)
        else:
            copy, reach = (s_copy, S_REACH) if what[0] == "S" else (x_copy, X_REACH)
            spread(copy, reach, int(what[1:]))

    systems = []
    big_row = lax.broadcasted_iota(jnp.int32, (72, 128), 0)
    big_lane = lax.broadcasted_iota(jnp.int32, (72, 128), 1)
    unit = jnp.where((big_row < 64) & (big_lane % 64 == big_row), 1.0, 0.0)
    for p in range(2):
        lefts, centres = [], []
        for odd in range(2):
            tiles = []
            for q in range(8):
                a = sz[q, 8 * p:8 * p + 8, :]
                b = sz[q + 8, 8 * p:8 * p + 8, :]
                if odd:
                    tiles.append(jnp.where(top, pltpu.roll(a, 4, 0), b))
                else:
                    tiles.append(jnp.where(top, a, pltpu.roll(b, 4, 0)))
            total = functools.reduce(jnp.add, tiles)
            mean = jnp.sum(total, axis=0, keepdims=True) * (1.0 / 64.0)
            centred = jnp.concatenate(tiles, axis=0) - mean
            centres.append(centred)
            lefts.append(jnp.concatenate([centred, obs_side[2 * p + odd]], axis=0))
        none = jnp.zeros_like(centres[0])
        left = jnp.concatenate(lefts, axis=1)
        right = jnp.concatenate([
            jnp.concatenate([centres[0], none], axis=1),
            jnp.concatenate([none, centres[1]], axis=1)], axis=0)
        gram = lax.dot_general(left, right, NT, precision=HIGHEST, preferred_element_type=f32)
        system = gram * (1.0 / 63.0) + unit
        systems.append([system[8 * t:8 * t + 8] for t in range(9)])
    solved = eliminate(systems)

    settle(x_copy, X_REACH)

    keep = top == (lax.rem(lane, 8) < 4)
    for i in range(BLK):
        t = -solved[i // 2]
        if i % 2 == 0:
            t = pltpu.roll(t, 64, 1)
        t = jnp.where(lane >= 64, t, 0.0)
        t = t - jnp.sum(t, axis=1, keepdims=True) * (1.0 / 64.0)
        coef = jnp.where(
            lane >= 64,
            jnp.where(top, pltpu.roll(t, 124, 1), t),
            jnp.where(top, pltpu.roll(t, 64, 1), pltpu.roll(t, 68, 1)))
        coef = jnp.where(keep, coef, 0.0)
        for s in (2 * i, 2 * i + 1):
            stored = xz[:, 8 * s:8 * s + 8, :].reshape(128, 128)
            new = xz[0, 8 * s:8 * s + 8, :] + jnp.dot(
                coef, stored, precision=HIGHEST, preferred_element_type=f32)
            an_v[pl.ds(4 * s + 1, 4, stride=32), :] = new[0:4]
            an_v[pl.ds(4 * s + 2, 4, stride=32), :] = new[4:8]
    for m in range(MEM):
        an_v[pl.ds(32 * m, 8, stride=4), :] = states[m][0]
        an_v[pl.ds(32 * m + 3, 8, stride=4), :] = states[m][3]

    for step in STEPS:
        g_copy(step).wait_send()
    for slot in range(1, NMEM):
        s_copy(0, slot, 1).wait_send()
        x_copy(0, slot, 1).wait_send()


def hand_over(an, q, an_out, q_out, sem):
    copies = [pltpu.make_async_copy(q, q_out, sem.at[0]), pltpu.make_async_copy(an, an_out, sem.at[1])]
    for cp in copies:
        cp.start()
    for cp in copies:
        cp.wait()


def on_device(init, prm, rain, temp, evap, meas, sig, draws, pos, flag, adj):
    def member_rows(a):
        return a.reshape(-1, 4, 8, 128).transpose(0, 2, 1, 3).reshape(-1, 128)

    def hour_rows(a):
        return a.reshape(3, 8, 8, 128).transpose(0, 2, 1, 3).reshape(192, 128)

    any_spec = pl.BlockSpec(memory_space=pl.ANY)
    hbm_spec = pl.BlockSpec(memory_space=pltpu.HBM)
    dma = pltpu.SemaphoreType.DMA
    an, q = pl.pallas_call(
        kernel,
        out_shape=(jax.ShapeDtypeStruct((128, 128), f32), jax.ShapeDtypeStruct((768, 128), f32)),
        in_specs=[hbm_spec] * 11,
        out_specs=(pl.BlockSpec(memory_space=pltpu.VMEM),) * 2,
        scratch_shapes=[
            pltpu.VMEM((128, 128), f32), pltpu.VMEM((10, 1024), f32), pltpu.VMEM((768, 128), f32),
            pltpu.VMEM((192, 128), f32), pltpu.VMEM((192, 128), f32),
            pltpu.VMEM((4, 32), f32), pltpu.VMEM((4, 32), f32), pltpu.VMEM((4, 4, 32), f32),
            pltpu.VMEM((4, 32), jnp.int32), pltpu.VMEM((4, 32), jnp.int32), pltpu.SMEM((3, 128), jnp.int32),
            pltpu.VMEM((80, 128), f32),
            pltpu.VMEM((1024, 128), jnp.bfloat16), pltpu.VMEM((128, 128), f32),
            pltpu.VMEM((32, 8, 128), f32), pltpu.VMEM((16, 16, 128), f32), pltpu.VMEM((16, 64, 128), f32),
            dma((11,)), dma((31,)), dma((31,)), dma((15,)), dma((15,)), dma((15,)), dma((15,)),
        ],
        compiler_params=pltpu.CompilerParams(collective_id=0, has_side_effects=True, vmem_limit_bytes=LIMIT),
    )(*[pltpu.with_memory_space_constraint(a, pltpu.HBM) for a in (
        member_rows(init), prm, member_rows(rain), hour_rows(temp), hour_rows(evap), meas, sig,
        draws.transpose(0, 2, 1), pos, flag, adj.T)])

    an, q = pl.pallas_call(
        hand_over,
        out_shape=(jax.ShapeDtypeStruct((128, 128), f32), jax.ShapeDtypeStruct((768, 128), f32)),
        in_specs=[any_spec] * 2,
        out_specs=(any_spec, any_spec),
        scratch_shapes=[dma((2,))],
        compiler_params=pltpu.CompilerParams(vmem_limit_bytes=LIMIT),
    )(an, q)

    def whole(a):
        return a.reshape(-1, 8, 4, 128).transpose(0, 2, 1, 3).reshape(-1, 4, 1024)

    return whole(an), whole(q)


def solution(mesh):
    placed = (
        P("member", None, "basin"),
        P(None, "basin"),
        P(None, "member", "basin"),
        P(None, "basin"),
        P(None, "basin"),
        P("basin", None),
        P("basin", None),
        P("basin", None, "member"),
        P("basin", None),
        P("basin", None),
        P(),
    )
    return jax.shard_map(
        on_device,
        mesh=mesh,
        in_specs=placed,
        out_specs=(P("member", None, "basin"), P(None, "member", "basin")),
        check_vma=False,
    )
```

```python
import functools
import math

import jax
import jax.numpy as jnp
from jax import lax
from jax.experimental import pallas as pl
from jax.experimental.pallas import tpu as pltpu
from jax.sharding import PartitionSpec as P

f32 = jnp.float32
NB = 256
OBS = 32
NBR = 3
BLK = 4
HOURS = 24
MEM = 4
NBAS = 32
NMEM = 16
X_SPANS = (3, 3, 2)
S_SPANS = (4, 4)
REACH = max(X_SPANS + S_SPANS)
ORDER = ('S', 'X', 'S', 'X', 'W')
LIMIT = 16 * 1024 * 1024

MESH = pl.DeviceIdType.MESH
HIGHEST = lax.Precision.HIGHEST
NT = (((1,), (1,)), ((), ()))
LOG2E = math.log2(math.e)

PARAM_LOW = (-1.5, 0.0002, 0.8, 1.0, 0.4, 0.01, 0.002, 0.0001, 0.1, 0.0001)
PARAM_HIGH = (1.5, 0.002, 4.0, 5.0, 1.0, 0.05, 0.02, 0.002, 0.5, 0.001)


STEPS = sorted(((dy, dx, dc) for dy in range(4) for dx in range(4) for dc in range(2)),
               key=lambda o: (-min(o[0], 4 - o[0]) - min(o[1], 4 - o[1]), -o[2]))[:-1]


def hour_step(states, rains, temp, evap, par):
    (thresh, melt_rate, field_cap, inv_cap, shape_log, inv_limit,
     quick_rate, upper_rate, lower_rate, upper_limit, percolation) = par
    share = jnp.clip((thresh + 1.0 - temp) * 0.5, 0.0, 1.0)
    dry = 1.0 - share
    melt_cap = melt_rate * jnp.maximum(temp - thresh, 0.0)
    out = []
    flows = []
    for (snow, moist, upper, lower), rain in zip(states, rains):
        snow = snow + share * rain
        melt = jnp.minimum(melt_cap, snow)
        snow = snow - melt
        inflow = dry * rain + melt
        recharge = inflow * jnp.exp2(shape_log * jnp.log(moist * inv_cap))
        moist = moist + inflow - recharge
        excess = jnp.maximum(moist - field_cap, 0.0)
        moist = moist - excess
        actual = jnp.minimum(evap * jnp.minimum(moist * inv_limit, 1.0), moist)
        moist = moist - actual
        upper = upper + recharge + excess
        perc = jnp.minimum(percolation, upper)
        upper = upper - perc
        lower = lower + perc
        quick = quick_rate * jnp.maximum(upper - upper_limit, 0.0)
        slow = upper_rate * upper
        base = lower_rate * lower
        upper = upper - quick - slow
        lower = lower - base
        out.append((snow, moist, upper, lower))
        flows.append(100.0 * (quick + slow + base))
    return out, flows


def eliminate(pairs):
    pairs = [list(b) for b in pairs]
    shape = (8, 128)
    lane = lax.broadcasted_iota(jnp.int32, shape, 1)
    half = lane - lane % 64

    def take(v, index, axis):
        return jnp.take_along_axis(v, index, axis=axis, mode="promise_in_bounds")

    for k in range(0, 64, 4):
        kt, kr = divmod(k, 8)
        here = [lane % 64 == k + j for j in range(4)]
        inside = (lane % 64 >= k) & (lane % 64 < k + 4)
        columns = [half + (k + j) for j in range(4)]
        for b in pairs:
            head = [take(b[kt], columns[j], 1) for j in range(4)]

            def at(i, j):
                return jnp.broadcast_to(head[j][kr + i:kr + i + 1, :], shape)

            r = [jnp.broadcast_to(b[kt][kr + j:kr + j + 1, :], shape) for j in range(4)]
            r = [jnp.where(inside, jnp.where(here[j], 1.0, 0.0), r[j]) for j in range(4)]
            a00, a01, b00, b01 = (at(0, j) for j in range(4))
            a11, b10, b11 = (at(1, j) for j in (1, 2, 3))
            d00, d01 = (at(2, j) for j in (2, 3))
            d11 = at(3, 3)
            inv = 1.0 / (a00 * a11 - a01 * a01)
            i00, i01, i11 = a11 * inv, -a01 * inv, a00 * inv
            g00, g01 = i00 * b00 + i01 * b10, i00 * b01 + i01 * b11
            g10, g11 = i01 * b00 + i11 * b10, i01 * b01 + i11 * b11
            s00 = d00 - (b00 * g00 + b10 * g10)
            s01 = d01 - (b00 * g01 + b10 * g11)
            s11 = d11 - (b01 * g01 + b11 * g11)
            jnv = 1.0 / (s00 * s11 - s01 * s01)
            q2 = r[2] - (g00 * r[0] + g10 * r[1])
            q3 = r[3] - (g01 * r[0] + g11 * r[1])
            n2 = (s11 * q2 - s01 * q3) * jnv
            n3 = (s00 * q3 - s01 * q2) * jnv
            n0 = i00 * r[0] + i01 * r[1] - (g00 * n2 + g01 * n3)
            n1 = i01 * r[0] + i11 * r[1] - (g10 * n2 + g11 * n3)
            for t in range(kt + kr // 4, 9):
                c = head if t == kt else [take(b[t], columns[j], 1) for j in range(4)]
                b[t] = jnp.where(inside, 0.0, b[t]) - ((c[0] * n0 + c[1] * n1) + (c[2] * n2 + c[3] * n3))
    return [b[8] for b in pairs]


def kernel(init, prm, rain, temp, evap, meas, sig, draws, pos, flag, adj_hbm, an_v, q_v,
           init_v, prm_v, rain_v, temp_v, evap_v, meas_v, sig_v, draws_v, pos_v, flag_v, adj,
           prow_v, oh_v, turn_v, gath, sz, xz,
           in_sem, gs_sem, gr_sem, ss_sem, sr_sem, xs_sem, xr_sem):
    me_b = lax.axis_index("basin")
    me_z = lax.axis_index("member")
    shape = (8, 128)
    lane = lax.broadcasted_iota(jnp.int32, shape, 1)
    row = lax.broadcasted_iota(jnp.int32, shape, 0)
    top = row < 4

    loads = []
    for src, dst in ((sig, sig_v), (flag, flag_v), (meas, meas_v), (draws, draws_v), (pos, pos_v),
                     (prm, prm_v), (temp, temp_v), (evap, evap_v), (init, init_v), (rain, rain_v), (adj_hbm, adj)):
        cp = pltpu.make_async_copy(src, dst, in_sem.at[len(loads)])
        cp.start()
        loads.append(cp)

    barrier = pltpu.get_barrier_semaphore()

    me_y, me_x, me_c = lax.div(me_b, 8), lax.rem(lax.div(me_b, 2), 4), lax.rem(me_b, 2)

    to_y = [lax.rem(me_y + d, 4) * 8 for d in range(4)]
    to_x = [lax.rem(me_x + d, 4) * 2 for d in range(4)]
    to_c = [lax.rem(me_c + d, 2) for d in range(2)]
    to_z = [lax.rem(me_z + d, NMEM) for d in range(NMEM)]

    def there(step):
        return {"basin": to_y[step[0]] + to_x[step[1]] + to_c[step[2]]}

    for step in STEPS:
        pl.semaphore_signal(barrier, inc=1, device_id=there(step), device_id_type=MESH)
    for d in range(1, REACH + 1):
        for to in {d, NMEM - d}:
            pl.semaphore_signal(barrier, inc=1, device_id={"member": to_z[to % NMEM]}, device_id_type=MESH)

    for cp in loads[:5]:
        cp.wait()

    weights, perts, places = [], [], []
    for i in range(BLK):
        sd = sig_v[i:i + 1, :]
        weights.append(jnp.broadcast_to(flag_v[i:i + 1, :].astype(f32) / sd, (8, OBS)))
        pert = meas_v[i:i + 1, :] + sd * draws_v[i]
        perts.append(jnp.concatenate([pert, pert], axis=0))
        places.append(jnp.broadcast_to(pos_v[i:i + 1, :] + NB * i, (8, OBS)))
    weight = jnp.concatenate(weights, axis=1)
    pert = jnp.concatenate(perts, axis=1)
    place = jnp.concatenate(places, axis=1)
    place16 = jnp.concatenate([place, place], axis=0)
    row16 = lax.broadcasted_iota(jnp.int32, (16, 128), 0)
    for j in range(64):
        oh_v[16 * j:16 * j + 16, :] = jnp.where(place16 == row16 + 16 * j, 1.0, 0.0).astype(jnp.bfloat16)

    loads[5].wait()
    par = []
    for s in range(8):
        prow_v[8 * s:8 * s + 8, :] = prm_v[0:8, 128 * s:128 * s + 128]
        prow_v[64 + 2 * s:66 + 2 * s, :] = prm_v[8:10, 128 * s:128 * s + 128]
    for k in range(10):
        v = prow_v[pl.ds(k, 8, stride=8), :] if k < 8 else prow_v[pl.ds(64 + k - 8, 8, stride=2), :]
        par.append(PARAM_LOW[k] + (PARAM_HIGH[k] - PARAM_LOW[k]) * v)
    tt, cfmax, fc, beta, lp, k0, k1, k2, uzl, perc = par
    inv_fc = 1.0 / fc
    hydro = (tt, cfmax, fc, inv_fc, beta * LOG2E, 1.0 / (lp * fc), k0, k1, k2, uzl, perc)

    for cp in loads[6:]:
        cp.wait()
    states = [tuple(init_v[pl.ds(32 * m + c, 8, stride=4), :] for c in range(4)) for m in range(MEM)]

    def eight_hours(chunk, states):
        flows = None
        for h in range(8):
            base = chunk * 256 + 32 * h
            rains = [rain_v[pl.ds(base + m, 8, stride=4), :] for m in range(MEM)]
            tmp = temp_v[pl.ds(chunk * 64 + h, 8, stride=8), :]
            eva = evap_v[pl.ds(chunk * 64 + h, 8, stride=8), :]
            states, flows = hour_step(states, rains, tmp, eva, hydro)
            for m in range(MEM):
                q_v[pl.ds(base + m, 8, stride=4), :] = flows[m]
        return states, flows

    states, flows = lax.fori_loop(
        0, 3, lambda c, s: eight_hours(c, s[0]),
        (states, [jnp.zeros(shape, f32)] * MEM))

    for m in range(MEM):
        turn_v[8 * m:8 * m + 8, :] = states[m][1]
        turn_v[32 + 8 * m:40 + 8 * m, :] = states[m][2]
    for s in range(8):
        xz[0, 8 * s:8 * s + 8, :] = turn_v[pl.ds(s, 8, stride=8), :]
    for m in range(MEM):
        turn_v[64 + 8 * m:72 + 8 * m, :] = flows[m]
        turn_v[96 + 8 * m:104 + 8 * m, :] = 0.45 * states[m][1] * inv_fc
    field = jnp.concatenate([turn_v[pl.ds(64 + s, 8, stride=8), :] for s in range(8)], axis=1)
    hi = field.astype(jnp.bfloat16).astype(f32)
    mid = (field - hi).astype(jnp.bfloat16).astype(f32)
    low = field - hi - mid
    stack = jnp.concatenate([hi, mid, low, jnp.zeros_like(low)], axis=0).astype(jnp.bfloat16)
    picked = jnp.dot(stack, oh_v[...], preferred_element_type=f32)
    both = picked[0:8] + picked[8:16] + picked[16:24]
    swapped = pltpu.roll(both, 4, 0)
    pred = jnp.where(top == (lax.rem(lane, OBS) < OBS // 2), both, swapped)
    tile = weight * jnp.where(top, pred, pert - pred)
    gath[0] = tile

    pl.semaphore_wait(barrier, NBAS - 1 + min(2 * REACH, NMEM - 1))

    def z_copy(buf, send, recv, src, slot, to):
        return pltpu.make_async_remote_copy(
            buf.at[src], buf.at[slot], send.at[slot - 1], recv.at[slot - 1],
            device_id={"member": to_z[to % NMEM]}, device_id_type=MESH)

    def x_copy(src, slot, to):
        return z_copy(xz, xs_sem, xr_sem, src, slot, to)

    def s_copy(src, slot, to):
        return z_copy(sz, ss_sem, sr_sem, src, slot, to)

    def spread(copy, spans, stage):
        base = sum(spans[:stage])
        if base:
            copy(0, base, 1).wait_recv()
            copy(0, NMEM - base, 1).wait_recv()
        for d in range(spans[stage], 0, -1):
            copy(base, base + d, d).start()
            if base + d < 8:
                copy((NMEM - base) % NMEM, NMEM - base - d, -d).start()

    def settle(copy, spans):
        relayed = [sum(spans[:stage]) for stage in range(1, len(spans))]
        for slot in range(1, NMEM):
            if min(slot, NMEM - slot) not in relayed:
                copy(0, slot, 1).wait_recv()

    def g_copy(step):
        slot = (step[0] * 4 + step[1]) * 2 + step[2]
        return pltpu.make_async_remote_copy(
            gath.at[0], gath.at[slot], gs_sem.at[slot - 1], gr_sem.at[slot - 1],
            device_id=there(step), device_id_type=MESH)

    for step in STEPS:
        g_copy(step).start()
    spread(x_copy, X_SPANS, 0)

    for m in range(MEM):
        an_v[pl.ds(32 * m, 8, stride=4), :] = states[m][0]
        an_v[pl.ds(32 * m + 3, 8, stride=4), :] = states[m][3]
    places = []
    for i in range(BLK):
        for j in range(NBR):
            n = adj[j, me_b * BLK + i]
            slot = (((me_y - (n >> 5)) & 3) * 8 + ((me_x - (n >> 3)) & 3) * 2 + ((me_c - (n >> 2)) & 1))
            places.append((slot, (OBS * (j + 1) - OBS * (n & 3)) & 127))
    for step in reversed(STEPS):
        g_copy(step).wait_recv()

    local = []
    for i in range(BLK):
        piece = tile if i == 0 else pltpu.roll(tile, 128 - OBS * i, 1)
        for j in range(NBR):
            slot, shift = places[i * NBR + j]
            far = pltpu.roll(gath[slot], shift, 1)
            piece = jnp.where(lax.div(lane, OBS) == j + 1, far, piece)
        local.append(piece)
    turned = [pltpu.roll(p, 4, 0) for p in local]
    for p in range(2):
        sz[0, 8 * p:8 * p + 8, :] = jnp.where(top, local[2 * p], turned[2 * p + 1])
    obs_side = [jnp.where(top, t, p) for t, p in zip(turned, local)]

    stage = {"S": 0, "X": 1}
    for what in ORDER:
        if what == "W":
            settle(s_copy, S_SPANS)
        elif what == "S":
            spread(s_copy, S_SPANS, stage[what])
            stage[what] += 1
        elif stage[what] < len(X_SPANS):
            spread(x_copy, X_SPANS, stage[what])
            stage[what] += 1

    systems = []
    big_row = lax.broadcasted_iota(jnp.int32, (72, 128), 0)
    big_lane = lax.broadcasted_iota(jnp.int32, (72, 128), 1)
    unit = jnp.where((big_row < 64) & (big_lane % 64 == big_row), 1.0, 0.0)
    for p in range(2):
        lefts, centres = [], []
        for odd in range(2):
            tiles = []
            for q in range(8):
                a = sz[q, 8 * p:8 * p + 8, :]
                b = sz[q + 8, 8 * p:8 * p + 8, :]
                if odd:
                    tiles.append(jnp.where(top, pltpu.roll(a, 4, 0), b))
                else:
                    tiles.append(jnp.where(top, a, pltpu.roll(b, 4, 0)))
            total = functools.reduce(jnp.add, tiles)
            mean = jnp.sum(total, axis=0, keepdims=True) * (1.0 / 64.0)
            centred = jnp.concatenate(tiles, axis=0) - mean
            centres.append(centred)
            lefts.append(jnp.concatenate([centred, obs_side[2 * p + odd]], axis=0))
        none = jnp.zeros_like(centres[0])
        left = jnp.concatenate(lefts, axis=1)
        right = jnp.concatenate([
            jnp.concatenate([centres[0], none], axis=1),
            jnp.concatenate([none, centres[1]], axis=1)], axis=0)
        gram = lax.dot_general(left, right, NT, precision=HIGHEST, preferred_element_type=f32)
        system = gram * (1.0 / 63.0) + unit
        systems.append([system[8 * t:8 * t + 8] for t in range(9)])
    solved = eliminate(systems)

    for step in STEPS:
        g_copy(step).wait_send()
    for slot in range(1, NMEM):
        s_copy(0, slot, 1).wait_send()
        x_copy(0, slot, 1).wait_send()
    settle(x_copy, X_SPANS)

    keep = top == (lax.rem(lane, 8) < 4)
    for i in range(BLK):
        t = -solved[i // 2]
        if i % 2 == 0:
            t = pltpu.roll(t, 64, 1)
        t = jnp.where(lane >= 64, t, 0.0)
        t = t - jnp.sum(t, axis=1, keepdims=True) * (1.0 / 64.0)
        coef = jnp.where(
            lane >= 64,
            jnp.where(top, pltpu.roll(t, 124, 1), t),
            jnp.where(top, pltpu.roll(t, 64, 1), pltpu.roll(t, 68, 1)))
        coef = jnp.where(keep, coef, 0.0)
        for s in (2 * i, 2 * i + 1):
            stored = xz[:, 8 * s:8 * s + 8, :].reshape(128, 128)
            new = xz[0, 8 * s:8 * s + 8, :] + jnp.dot(
                coef, stored, precision=HIGHEST, preferred_element_type=f32)
            an_v[pl.ds(4 * s + 1, 4, stride=32), :] = new[0:4]
            an_v[pl.ds(4 * s + 2, 4, stride=32), :] = new[4:8]


def hand_over(an, q, an_out, q_out, sem):
    copies = [pltpu.make_async_copy(q, q_out, sem.at[0]), pltpu.make_async_copy(an, an_out, sem.at[1])]
    for cp in copies:
        cp.start()
    for cp in copies:
        cp.wait()


def on_device(init, prm, rain, temp, evap, meas, sig, draws, pos, flag, adj):
    def member_rows(a):
        return a.reshape(-1, 4, 8, 128).transpose(0, 2, 1, 3).reshape(-1, 128)

    def hour_rows(a):
        return a.reshape(3, 8, 8, 128).transpose(0, 2, 1, 3).reshape(192, 128)

    any_spec = pl.BlockSpec(memory_space=pl.ANY)
    hbm_spec = pl.BlockSpec(memory_space=pltpu.HBM)
    dma = pltpu.SemaphoreType.DMA
    an, q = pl.pallas_call(
        kernel,
        out_shape=(jax.ShapeDtypeStruct((128, 128), f32), jax.ShapeDtypeStruct((768, 128), f32)),
        in_specs=[hbm_spec] * 11,
        out_specs=(pl.BlockSpec(memory_space=pltpu.VMEM),) * 2,
        scratch_shapes=[
            pltpu.VMEM((128, 128), f32), pltpu.VMEM((10, 1024), f32), pltpu.VMEM((768, 128), f32),
            pltpu.VMEM((192, 128), f32), pltpu.VMEM((192, 128), f32),
            pltpu.VMEM((4, 32), f32), pltpu.VMEM((4, 32), f32), pltpu.VMEM((4, 4, 32), f32),
            pltpu.VMEM((4, 32), jnp.int32), pltpu.VMEM((4, 32), jnp.int32), pltpu.SMEM((3, 128), jnp.int32),
            pltpu.VMEM((80, 128), f32),
            pltpu.VMEM((1024, 128), jnp.bfloat16), pltpu.VMEM((128, 128), f32),
            pltpu.VMEM((32, 8, 128), f32), pltpu.VMEM((16, 16, 128), f32), pltpu.VMEM((16, 64, 128), f32),
            dma((11,)), dma((31,)), dma((31,)), dma((15,)), dma((15,)), dma((15,)), dma((15,)),
        ],
        compiler_params=pltpu.CompilerParams(collective_id=0, has_side_effects=True, vmem_limit_bytes=LIMIT),
    )(*[pltpu.with_memory_space_constraint(a, pltpu.HBM) for a in (
        member_rows(init), prm, member_rows(rain), hour_rows(temp), hour_rows(evap), meas, sig,
        draws.transpose(0, 2, 1), pos, flag, adj.T)])

    an, q = pl.pallas_call(
        hand_over,
        out_shape=(jax.ShapeDtypeStruct((128, 128), f32), jax.ShapeDtypeStruct((768, 128), f32)),
        in_specs=[any_spec] * 2,
        out_specs=(any_spec, any_spec),
        scratch_shapes=[dma((2,))],
        compiler_params=pltpu.CompilerParams(vmem_limit_bytes=LIMIT),
    )(an, q)

    def whole(a):
        return a.reshape(-1, 8, 4, 128).transpose(0, 2, 1, 3).reshape(-1, 4, 1024)

    return whole(an), whole(q)


def solution(mesh):
    placed = (
        P("member", None, "basin"),
        P(None, "basin"),
        P(None, "member", "basin"),
        P(None, "basin"),
        P(None, "basin"),
        P("basin", None),
        P("basin", None),
        P("basin", None, "member"),
        P("basin", None),
        P("basin", None),
        P(),
    )
    return jax.shard_map(
        on_device,
        mesh=mesh,
        in_specs=placed,
        out_specs=(P("member", None, "basin"), P(None, "member", "basin")),
        check_vma=False,
    )
```

```python
import functools
import math

import jax
import jax.numpy as jnp
from jax import lax
from jax.experimental import pallas as pl
from jax.experimental.pallas import tpu as pltpu
from jax.sharding import PartitionSpec as P

f32 = jnp.float32
NB = 256
OBS = 32
NBR = 3
BLK = 4
HOURS = 24
MEM = 4
NBAS = 32
NMEM = 16
X_SPANS = (3, 3, 2)
S_SPANS = (4, 4)
REACH = max(X_SPANS + S_SPANS)
ORDER = ('S', 'X', 'S', 'X', 'W')
LIMIT = 16 * 1024 * 1024

MESH = pl.DeviceIdType.MESH
HIGHEST = lax.Precision.HIGHEST
NT = (((1,), (1,)), ((), ()))
LOG2E = math.log2(math.e)

PARAM_LOW = (-1.5, 0.0002, 0.8, 1.0, 0.4, 0.01, 0.002, 0.0001, 0.1, 0.0001)
PARAM_HIGH = (1.5, 0.002, 4.0, 5.0, 1.0, 0.05, 0.02, 0.002, 0.5, 0.001)


STEPS = sorted(((dy, dx, dc) for dy in range(4) for dx in range(4) for dc in range(2)),
               key=lambda o: (-min(o[0], 4 - o[0]) - min(o[1], 4 - o[1]), -o[2]))[:-1]


def hour_step(states, rains, temp, evap, par):
    (thresh, melt_rate, field_cap, inv_cap, shape_log, inv_limit,
     quick_rate, upper_rate, lower_rate, upper_limit, percolation) = par
    share = jnp.clip((thresh + 1.0 - temp) * 0.5, 0.0, 1.0)
    dry = 1.0 - share
    melt_cap = melt_rate * jnp.maximum(temp - thresh, 0.0)
    out = []
    flows = []
    for (snow, moist, upper, lower), rain in zip(states, rains):
        snow = snow + share * rain
        melt = jnp.minimum(melt_cap, snow)
        snow = snow - melt
        inflow = dry * rain + melt
        recharge = inflow * jnp.exp2(shape_log * jnp.log(moist * inv_cap))
        moist = moist + inflow - recharge
        excess = jnp.maximum(moist - field_cap, 0.0)
        moist = moist - excess
        actual = jnp.minimum(evap * jnp.minimum(moist * inv_limit, 1.0), moist)
        moist = moist - actual
        upper = upper + recharge + excess
        perc = jnp.minimum(percolation, upper)
        upper = upper - perc
        lower = lower + perc
        quick = quick_rate * jnp.maximum(upper - upper_limit, 0.0)
        slow = upper_rate * upper
        base = lower_rate * lower
        upper = upper - quick - slow
        lower = lower - base
        out.append((snow, moist, upper, lower))
        flows.append(100.0 * (quick + slow + base))
    return out, flows


def eliminate(pairs):
    pairs = [list(b) for b in pairs]
    shape = (8, 128)
    lane = lax.broadcasted_iota(jnp.int32, shape, 1)
    half = lane - lane % 64

    def take(v, index, axis):
        return jnp.take_along_axis(v, index, axis=axis, mode="promise_in_bounds")

    for k in range(0, 64, 4):
        kt, kr = divmod(k, 8)
        here = [lane % 64 == k + j for j in range(4)]
        inside = (lane % 64 >= k) & (lane % 64 < k + 4)
        columns = [half + (k + j) for j in range(4)]
        for b in pairs:
            head = [take(b[kt], columns[j], 1) for j in range(4)]

            def at(i, j):
                return jnp.broadcast_to(head[j][kr + i:kr + i + 1, :], shape)

            r = [jnp.broadcast_to(b[kt][kr + j:kr + j + 1, :], shape) for j in range(4)]
            r = [jnp.where(inside, jnp.where(here[j], 1.0, 0.0), r[j]) for j in range(4)]
            a00, a01, b00, b01 = (at(0, j) for j in range(4))
            a11, b10, b11 = (at(1, j) for j in (1, 2, 3))
            d00, d01 = (at(2, j) for j in (2, 3))
            d11 = at(3, 3)
            inv = 1.0 / (a00 * a11 - a01 * a01)
            i00, i01, i11 = a11 * inv, -a01 * inv, a00 * inv
            g00, g01 = i00 * b00 + i01 * b10, i00 * b01 + i01 * b11
            g10, g11 = i01 * b00 + i11 * b10, i01 * b01 + i11 * b11
            s00 = d00 - (b00 * g00 + b10 * g10)
            s01 = d01 - (b00 * g01 + b10 * g11)
            s11 = d11 - (b01 * g01 + b11 * g11)
            jnv = 1.0 / (s00 * s11 - s01 * s01)
            q2 = r[2] - (g00 * r[0] + g10 * r[1])
            q3 = r[3] - (g01 * r[0] + g11 * r[1])
            n2 = (s11 * q2 - s01 * q3) * jnv
            n3 = (s00 * q3 - s01 * q2) * jnv
            n0 = i00 * r[0] + i01 * r[1] - (g00 * n2 + g01 * n3)
            n1 = i01 * r[0] + i11 * r[1] - (g10 * n2 + g11 * n3)
            for t in range(kt + kr // 4, 9):
                c = head if t == kt else [take(b[t], columns[j], 1) for j in range(4)]
                b[t] = jnp.where(inside, 0.0, b[t]) - ((c[0] * n0 + c[1] * n1) + (c[2] * n2 + c[3] * n3))
    return [b[8] for b in pairs]


def kernel(init, prm, rain, temp, evap, meas, sig, draws, pos, flag, adj_hbm, an_v, q_v,
           init_v, prm_v, rain_v, temp_v, evap_v, meas_v, sig_v, draws_v, pos_v, flag_v, adj,
           prow_v, oh_v, turn_v, gath, sz, xz,
           in_sem, gs_sem, gr_sem, ss_sem, sr_sem, xs_sem, xr_sem):
    me_b = lax.axis_index("basin")
    me_z = lax.axis_index("member")
    shape = (8, 128)
    lane = lax.broadcasted_iota(jnp.int32, shape, 1)
    row = lax.broadcasted_iota(jnp.int32, shape, 0)
    top = row < 4

    loads = []
    for src, dst in ((sig, sig_v), (flag, flag_v), (meas, meas_v), (draws, draws_v), (pos, pos_v),
                     (prm, prm_v), (temp, temp_v), (evap, evap_v), (init, init_v), (rain, rain_v), (adj_hbm, adj)):
        cp = pltpu.make_async_copy(src, dst, in_sem.at[len(loads)])
        cp.start()
        loads.append(cp)

    barrier = pltpu.get_barrier_semaphore()

    me_y, me_x, me_c = lax.div(me_b, 8), lax.rem(lax.div(me_b, 2), 4), lax.rem(me_b, 2)

    to_y = [lax.rem(me_y + d, 4) * 8 for d in range(4)]
    to_x = [lax.rem(me_x + d, 4) * 2 for d in range(4)]
    to_c = [lax.rem(me_c + d, 2) for d in range(2)]
    to_z = [lax.rem(me_z + d, NMEM) for d in range(NMEM)]

    def there(step):
        return {"basin": to_y[step[0]] + to_x[step[1]] + to_c[step[2]]}

    for step in STEPS:
        pl.semaphore_signal(barrier, inc=1, device_id=there(step), device_id_type=MESH)
    for d in range(1, REACH + 1):
        for to in {d, NMEM - d}:
            pl.semaphore_signal(barrier, inc=1, device_id={"member": to_z[to % NMEM]}, device_id_type=MESH)

    for cp in loads[:5]:
        cp.wait()

    weights, perts, places = [], [], []
    for i in range(BLK):
        sd = sig_v[i:i + 1, :]
        weights.append(jnp.broadcast_to(flag_v[i:i + 1, :].astype(f32) / sd, (8, OBS)))
        pert = meas_v[i:i + 1, :] + sd * draws_v[i]
        perts.append(jnp.concatenate([pert, pert], axis=0))
        places.append(jnp.broadcast_to(pos_v[i:i + 1, :] + NB * i, (8, OBS)))
    weight = jnp.concatenate(weights, axis=1)
    pert = jnp.concatenate(perts, axis=1)
    place = jnp.concatenate(places, axis=1)
    place16 = jnp.concatenate([place, place], axis=0)
    row16 = lax.broadcasted_iota(jnp.int32, (16, 128), 0)
    for j in range(64):
        oh_v[16 * j:16 * j + 16, :] = jnp.where(place16 == row16 + 16 * j, 1.0, 0.0).astype(jnp.bfloat16)

    loads[5].wait()
    par = []
    for s in range(8):
        prow_v[8 * s:8 * s + 8, :] = prm_v[0:8, 128 * s:128 * s + 128]
        prow_v[64 + 2 * s:66 + 2 * s, :] = prm_v[8:10, 128 * s:128 * s + 128]
    for k in range(10):
        v = prow_v[pl.ds(k, 8, stride=8), :] if k < 8 else prow_v[pl.ds(64 + k - 8, 8, stride=2), :]
        par.append(PARAM_LOW[k] + (PARAM_HIGH[k] - PARAM_LOW[k]) * v)
    tt, cfmax, fc, beta, lp, k0, k1, k2, uzl, perc = par
    inv_fc = 1.0 / fc
    hydro = (tt, cfmax, fc, inv_fc, beta * LOG2E, 1.0 / (lp * fc), k0, k1, k2, uzl, perc)

    for cp in loads[6:]:
        cp.wait()
    states = [tuple(init_v[pl.ds(32 * m + c, 8, stride=4), :] for c in range(4)) for m in range(MEM)]

    def eight_hours(chunk, states):
        flows = None
        for h in range(8):
            base = chunk * 256 + 32 * h
            rains = [rain_v[pl.ds(base + m, 8, stride=4), :] for m in range(MEM)]
            tmp = temp_v[pl.ds(chunk * 64 + h, 8, stride=8), :]
            eva = evap_v[pl.ds(chunk * 64 + h, 8, stride=8), :]
            states, flows = hour_step(states, rains, tmp, eva, hydro)
            for m in range(MEM):
                q_v[pl.ds(base + m, 8, stride=4), :] = flows[m]
        return states, flows

    states, flows = lax.fori_loop(
        0, 3, lambda c, s: eight_hours(c, s[0]),
        (states, [jnp.zeros(shape, f32)] * MEM))

    for m in range(MEM):
        turn_v[8 * m:8 * m + 8, :] = states[m][1]
        turn_v[32 + 8 * m:40 + 8 * m, :] = states[m][2]
    for s in range(8):
        xz[0, 8 * s:8 * s + 8, :] = turn_v[pl.ds(s, 8, stride=8), :]
    for m in range(MEM):
        turn_v[64 + 8 * m:72 + 8 * m, :] = flows[m]
        turn_v[96 + 8 * m:104 + 8 * m, :] = 0.45 * states[m][1] * inv_fc
    field = jnp.concatenate([turn_v[pl.ds(64 + s, 8, stride=8), :] for s in range(8)], axis=1)
    hi = field.astype(jnp.bfloat16).astype(f32)
    mid = (field - hi).astype(jnp.bfloat16).astype(f32)
    low = field - hi - mid
    stack = jnp.concatenate([hi, mid, low, jnp.zeros_like(low)], axis=0).astype(jnp.bfloat16)
    picked = jnp.dot(stack, oh_v[...], preferred_element_type=f32)
    both = picked[0:8] + picked[8:16] + picked[16:24]
    swapped = pltpu.roll(both, 4, 0)
    pred = jnp.where(top == (lax.rem(lane, OBS) < OBS // 2), both, swapped)
    tile = weight * jnp.where(top, pred, pert - pred)
    gath[0] = tile

    pl.semaphore_wait(barrier, NBAS - 1 + min(2 * REACH, NMEM - 1))

    def z_copy(buf, send, recv, src, slot, to):
        return pltpu.make_async_remote_copy(
            buf.at[src], buf.at[slot], send.at[slot - 1], recv.at[slot - 1],
            device_id={"member": to_z[to % NMEM]}, device_id_type=MESH)

    def x_copy(src, slot, to):
        return z_copy(xz, xs_sem, xr_sem, src, slot, to)

    def s_copy(src, slot, to):
        return z_copy(sz, ss_sem, sr_sem, src, slot, to)

    def spread(copy, spans, stage):
        base = sum(spans[:stage])
        if base:
            copy(0, base, 1).wait_recv()
        for d in range(spans[stage], 0, -1):
            copy(base, base + d, d).start()
        if base:
            copy(0, NMEM - base, 1).wait_recv()
        for d in range(spans[stage], 0, -1):
            if base + d < 8:
                copy((NMEM - base) % NMEM, NMEM - base - d, -d).start()

    def settle(copy, spans):
        relayed = [sum(spans[:stage]) for stage in range(1, len(spans))]
        for slot in range(1, NMEM):
            if min(slot, NMEM - slot) not in relayed:
                copy(0, slot, 1).wait_recv()

    def g_copy(step):
        slot = (step[0] * 4 + step[1]) * 2 + step[2]
        return pltpu.make_async_remote_copy(
            gath.at[0], gath.at[slot], gs_sem.at[slot - 1], gr_sem.at[slot - 1],
            device_id=there(step), device_id_type=MESH)

    for step in STEPS:
        g_copy(step).start()
    spread(x_copy, X_SPANS, 0)

    for m in range(MEM):
        an_v[pl.ds(32 * m, 8, stride=4), :] = states[m][0]
        an_v[pl.ds(32 * m + 3, 8, stride=4), :] = states[m][3]
    places = []
    for i in range(BLK):
        for j in range(NBR):
            n = adj[j, me_b * BLK + i]
            slot = (((me_y - (n >> 5)) & 3) * 8 + ((me_x - (n >> 3)) & 3) * 2 + ((me_c - (n >> 2)) & 1))
            places.append((slot, (OBS * (j + 1) - OBS * (n & 3)) & 127))
    for step in reversed(STEPS):
        g_copy(step).wait_recv()

    local = []
    for i in range(BLK):
        piece = tile if i == 0 else pltpu.roll(tile, 128 - OBS * i, 1)
        for j in range(NBR):
            slot, shift = places[i * NBR + j]
            far = pltpu.roll(gath[slot], shift, 1)
            piece = jnp.where(lax.div(lane, OBS) == j + 1, far, piece)
        local.append(piece)
    turned = [pltpu.roll(p, 4, 0) for p in local]
    for p in range(2):
        sz[0, 8 * p:8 * p + 8, :] = jnp.where(top, local[2 * p], turned[2 * p + 1])
    obs_side = [jnp.where(top, t, p) for t, p in zip(turned, local)]

    stage = {"S": 0, "X": 1}
    for what in ORDER:
        if what == "W":
            settle(s_copy, S_SPANS)
        elif what == "S":
            spread(s_copy, S_SPANS, stage[what])
            stage[what] += 1
        elif stage[what] < len(X_SPANS):
            spread(x_copy, X_SPANS, stage[what])
            stage[what] += 1

    systems = []
    big_row = lax.broadcasted_iota(jnp.int32, (72, 128), 0)
    big_lane = lax.broadcasted_iota(jnp.int32, (72, 128), 1)
    unit = jnp.where((big_row < 64) & (big_lane % 64 == big_row), 1.0, 0.0)
    for p in range(2):
        lefts, centres = [], []
        for odd in range(2):
            tiles = []
            for q in range(8):
                a = sz[q, 8 * p:8 * p + 8, :]
                b = sz[q + 8, 8 * p:8 * p + 8, :]
                if odd:
                    tiles.append(jnp.where(top, pltpu.roll(a, 4, 0), b))
                else:
                    tiles.append(jnp.where(top, a, pltpu.roll(b, 4, 0)))
            total = functools.reduce(jnp.add, tiles)
            mean = jnp.sum(total, axis=0, keepdims=True) * (1.0 / 64.0)
            centred = jnp.concatenate(tiles, axis=0) - mean
            centres.append(centred)
            lefts.append(jnp.concatenate([centred, obs_side[2 * p + odd]], axis=0))
        none = jnp.zeros_like(centres[0])
        left = jnp.concatenate(lefts, axis=1)
        right = jnp.concatenate([
            jnp.concatenate([centres[0], none], axis=1),
            jnp.concatenate([none, centres[1]], axis=1)], axis=0)
        gram = lax.dot_general(left, right, NT, precision=HIGHEST, preferred_element_type=f32)
        system = gram * (1.0 / 63.0) + unit
        systems.append([system[8 * t:8 * t + 8] for t in range(9)])
    solved = eliminate(systems)

    for step in STEPS:
        g_copy(step).wait_send()
    for slot in range(1, NMEM):
        s_copy(0, slot, 1).wait_send()
        x_copy(0, slot, 1).wait_send()
    settle(x_copy, X_SPANS)

    keep = top == (lax.rem(lane, 8) < 4)
    for i in range(BLK):
        t = -solved[i // 2]
        if i % 2 == 0:
            t = pltpu.roll(t, 64, 1)
        t = jnp.where(lane >= 64, t, 0.0)
        t = t - jnp.sum(t, axis=1, keepdims=True) * (1.0 / 64.0)
        coef = jnp.where(
            lane >= 64,
            jnp.where(top, pltpu.roll(t, 124, 1), t),
            jnp.where(top, pltpu.roll(t, 64, 1), pltpu.roll(t, 68, 1)))
        coef = jnp.where(keep, coef, 0.0)
        coef_high = coef.astype(jnp.bfloat16).astype(f32)
        factors = jnp.concatenate([coef_high, coef - coef_high], axis=0).astype(jnp.bfloat16)
        for s in (2 * i, 2 * i + 1):
            stored = xz[:, 8 * s:8 * s + 8, :].reshape(128, 128)
            high = stored.astype(jnp.bfloat16)
            rest = (stored - high.astype(f32)).astype(jnp.bfloat16)
            first = jnp.dot(factors, high, preferred_element_type=f32)
            second = jnp.dot(factors, rest, preferred_element_type=f32)
            new = xz[0, 8 * s:8 * s + 8, :] + (first[0:8] + (first[8:16] + second[0:8]))
            an_v[pl.ds(4 * s + 1, 4, stride=32), :] = new[0:4]
            an_v[pl.ds(4 * s + 2, 4, stride=32), :] = new[4:8]


def hand_over(an, q, an_out, q_out, sem):
    copies = [pltpu.make_async_copy(q, q_out, sem.at[0]), pltpu.make_async_copy(an, an_out, sem.at[1])]
    for cp in copies:
        cp.start()
    for cp in copies:
        cp.wait()


def on_device(init, prm, rain, temp, evap, meas, sig, draws, pos, flag, adj):
    def member_rows(a):
        return a.reshape(-1, 4, 8, 128).transpose(0, 2, 1, 3).reshape(-1, 128)

    def hour_rows(a):
        return a.reshape(3, 8, 8, 128).transpose(0, 2, 1, 3).reshape(192, 128)

    any_spec = pl.BlockSpec(memory_space=pl.ANY)
    hbm_spec = pl.BlockSpec(memory_space=pltpu.HBM)
    dma = pltpu.SemaphoreType.DMA
    an, q = pl.pallas_call(
        kernel,
        out_shape=(jax.ShapeDtypeStruct((128, 128), f32), jax.ShapeDtypeStruct((768, 128), f32)),
        in_specs=[hbm_spec] * 11,
        out_specs=(pl.BlockSpec(memory_space=pltpu.VMEM),) * 2,
        scratch_shapes=[
            pltpu.VMEM((128, 128), f32), pltpu.VMEM((10, 1024), f32), pltpu.VMEM((768, 128), f32),
            pltpu.VMEM((192, 128), f32), pltpu.VMEM((192, 128), f32),
            pltpu.VMEM((4, 32), f32), pltpu.VMEM((4, 32), f32), pltpu.VMEM((4, 4, 32), f32),
            pltpu.VMEM((4, 32), jnp.int32), pltpu.VMEM((4, 32), jnp.int32), pltpu.SMEM((3, 128), jnp.int32),
            pltpu.VMEM((80, 128), f32),
            pltpu.VMEM((1024, 128), jnp.bfloat16), pltpu.VMEM((128, 128), f32),
            pltpu.VMEM((32, 8, 128), f32), pltpu.VMEM((16, 16, 128), f32), pltpu.VMEM((16, 64, 128), f32),
            dma((11,)), dma((31,)), dma((31,)), dma((15,)), dma((15,)), dma((15,)), dma((15,)),
        ],
        compiler_params=pltpu.CompilerParams(collective_id=0, has_side_effects=True, vmem_limit_bytes=LIMIT),
    )(*[pltpu.with_memory_space_constraint(a, pltpu.HBM) for a in (
        member_rows(init), prm, member_rows(rain), hour_rows(temp), hour_rows(evap), meas, sig,
        draws.transpose(0, 2, 1), pos, flag, adj.T)])

    an, q = pl.pallas_call(
        hand_over,
        out_shape=(jax.ShapeDtypeStruct((128, 128), f32), jax.ShapeDtypeStruct((768, 128), f32)),
        in_specs=[any_spec] * 2,
        out_specs=(any_spec, any_spec),
        scratch_shapes=[dma((2,))],
        compiler_params=pltpu.CompilerParams(vmem_limit_bytes=LIMIT),
    )(an, q)

    def whole(a):
        return a.reshape(-1, 8, 4, 128).transpose(0, 2, 1, 3).reshape(-1, 4, 1024)

    return whole(an), whole(q)


def solution(mesh):
    placed = (
        P("member", None, "basin"),
        P(None, "basin"),
        P(None, "member", "basin"),
        P(None, "basin"),
        P(None, "basin"),
        P("basin", None),
        P("basin", None),
        P("basin", None, "member"),
        P("basin", None),
        P("basin", None),
        P(),
    )
    return jax.shard_map(
        on_device,
        mesh=mesh,
        in_specs=placed,
        out_specs=(P("member", None, "basin"), P(None, "member", "basin")),
        check_vma=False,
    )
```
